128 devices in a mesh: ctx: 64 (over x_lo, y, z, core), head: 2 (over x_hi).
Axes of the slice: x: 4 (x_hi: 2, x_lo: 2; x = x_hi * 2 + x_lo), y: 4, z: 4, core: 2. Of those that a mesh axis runs over, the one named last changes fastest.
Arguments:
- queries: bfloat16 [32768, 1024], P(('ctx', 'head')), may hold values from -9 to 9
- keys_in: bfloat16 [32768, 1024], P(('ctx', 'head')), may hold values from -9 to 9
- values: bfloat16 [32768, 1024], P(('ctx', 'head')), may hold values from -6 to 6
- d_out: bfloat16 [32768, 1024], P(('ctx', 'head')), may hold values from -6 to 6
- pair_blocks: int32 [512, 16], replicated, may hold values from 0 to 511, as said below
- pair_count: int32 [512], replicated, may hold values from 1 to 16, as said below
Outputs:
- d_queries: bfloat16 [32768, 1024], P(('ctx', 'head'))
- d_keys: bfloat16 [32768, 1024], P(('ctx', 'head'))
- d_values: bfloat16 [32768, 1024], P(('ctx', 'head'))
The draws below stay inside these ranges and needn't reach their ends.
Inputs may be any that keep to these rules, and one draw needn't show every extreme that they name: `pair_blocks`: entry 0 of row b is b itself; every entry of row b is a block of a person within 2 persons of the person of block b (a person's tokens are 512 in a row). Entries may repeat. Only the first pair_count[b] entries of row b are listed.
All inputs are finite; a program needn't handle non-finite values.
Results may differ from the reference program's by a relative error of at most 0.012.
The reference program's roundings to bfloat16 on the way (of `probs_b` and `d_scores`) count: a program that leaves them out, or rounds other values in their place, can miss the bound.
Values may be sent and summed in bfloat16 or wider, within the bound.
A program may use at most 192 MiB of HBM per device.

```python
import jax
import jax.numpy as jnp
from jax import lax

HEADS = 16
HEAD_DIM = 64
FRAMES = 512
BLOCK = 64
REACH = 2
PAIRS = 16
PERSONS = 64
FEATURES = 1024
TOKENS = 32768


def query_key_pair(key):
    array_shape = (TOKENS, FEATURES)
    query_key = jax.random.fold_in(key, 101)
    key_key = jax.random.fold_in(key, 102)
    query_draw = jnp.clip(jax.random.normal(query_key, array_shape), -6.0, 6.0)
    key_draw = jnp.clip(jax.random.normal(key_key, array_shape), -6.0, 6.0)
    return (query_draw, key_draw)


def draw_queries(key, part):
    return query_key_pair(key)[0].astype(jnp.bfloat16)


def draw_keys_in(key, part):
    return query_key_pair(key)[1].astype(jnp.bfloat16)


def draw_pair_blocks(key, part):
    per_person = FRAMES // BLOCK
    total_blocks = PERSONS * per_person
    window_blocks = (2 * REACH + 1) * per_person
    block_ids = jnp.arange(total_blocks, dtype=jnp.int32)
    block_keys = jax.random.split(key, total_blocks)

    def one_block(block_key, block_id):
        person = block_id // per_person
        chosen_slots = jax.random.permutation(block_key, window_blocks - 1)[:PAIRS - 1].astype(jnp.int32)
        self_spot = REACH * per_person + block_id % per_person
        position = chosen_slots + (chosen_slots >= self_spot).astype(jnp.int32)
        offset = position // per_person - REACH
        target = person + offset
        offset = jnp.where((target < 0) | (target >= PERSONS), -offset, offset)
        picked = (person + offset) * per_person + position % per_person
        return jnp.concatenate([block_id[None], picked]).astype(jnp.int32)
    return jax.vmap(one_block)(block_keys, block_ids)


def draw_pair_count(key, part):
    per_person = FRAMES // BLOCK
    total_blocks = PERSONS * per_person
    busy_level = jax.random.randint(jax.random.fold_in(key, 1), (PERSONS,), 1, 5)
    drawn = jax.random.randint(jax.random.fold_in(key, 2), (total_blocks,), 1, PAIRS + 1)
    count_cap = jnp.maximum(1, busy_level * PAIRS // 4)
    counts = jnp.minimum(drawn, jnp.repeat(count_cap, per_person, total_repeat_length=total_blocks))
    full_block = jax.random.randint(jax.random.fold_in(key, 3), (), 0, total_blocks)
    return jnp.where(jnp.arange(total_blocks) == full_block, PAIRS, counts).astype(jnp.int32)


def block_scale(own_key, shape, shards, least, high):
    def one(dim, shards_of):
        heights = jax.random.uniform(jax.random.fold_in(jax.random.fold_in(own_key, 6), dim), (shards_of,), jnp.float32, least / len(shards), high / len(shards))
        return jnp.repeat(jnp.exp(heights), shape[dim] // shards_of).reshape((-1,) + (1,) * (len(shape) - dim - 1))

    factor_of = one(*shards[0])
    for cut in shards[1:]:
        factor_of = factor_of * one(*cut)
    return factor_of


def centred(own_key, dims, spread, bound, shards=(), kind=jnp.bfloat16):
    loudness = block_scale(own_key, dims, shards, -0.22, 0.18) if shards else 1.0
    result = jax.random.normal(own_key, dims, jnp.float32) * spread * loudness
    return jnp.minimum(jnp.maximum(result, -bound), bound).astype(kind)


def setup_inputs(seed: int = 0) -> dict:
    keys = jax.random.split(jax.random.key(seed), 7)
    queries = draw_queries(jax.random.fold_in(keys[6], 71), 0)
    keys_in = draw_keys_in(jax.random.fold_in(keys[6], 71), 0)
    values = centred(keys[2], (TOKENS, FEATURES), 1.0, 6.0, ((0, 128),))
    d_out = centred(keys[3], (TOKENS, FEATURES), 1.0, 6.0, ((0, 128),))
    pair_blocks = draw_pair_blocks(jax.random.fold_in(keys[6], 71), 0)
    pair_count = draw_pair_count(jax.random.fold_in(keys[6], 71), 0)
    return dict(queries=queries, keys_in=keys_in, values=values, d_out=d_out, pair_blocks=pair_blocks, pair_count=pair_count)


masked_value = -1.0e30


def reference(queries, keys_in, values, d_out, pair_blocks, pair_count):
    blocks_person = FRAMES // BLOCK
    window_span = 2 * REACH + 1
    window_rows = window_span * FRAMES
    margin = REACH * FRAMES
    score_scale = HEAD_DIM ** -0.5
    key_pad = jnp.pad(keys_in, ((margin, margin), (0, 0)))
    value_pad = jnp.pad(values, ((margin, margin), (0, 0)))
    live_slots = jnp.arange(PAIRS, dtype=jnp.int32)[None, :] < pair_count[:, None]

    def split_heads(matrix):
        return matrix.reshape(matrix.shape[0], HEADS, HEAD_DIM).astype(jnp.float32)

    def person_step(running, person):
        key_grad, value_grad = running
        start = (person * FRAMES).astype(jnp.int32)
        query_heads = split_heads(lax.dynamic_slice_in_dim(queries, start, FRAMES, 0))
        dout_heads = split_heads(lax.dynamic_slice_in_dim(d_out, start, FRAMES, 0))
        key_heads = split_heads(lax.dynamic_slice_in_dim(key_pad, start, window_rows, 0))
        value_heads = split_heads(lax.dynamic_slice_in_dim(value_pad, start, window_rows, 0))
        first = (person * blocks_person).astype(jnp.int32)
        lists = lax.dynamic_slice_in_dim(pair_blocks, first, blocks_person, 0)
        alive = lax.dynamic_slice_in_dim(live_slots, first, blocks_person, 0)
        wanted = ((person - REACH) * blocks_person).astype(jnp.int32) + jnp.arange(window_span * blocks_person, dtype=jnp.int32)
        block_mask = jnp.any((lists[:, :, None] == wanted[None, None, :]) & alive[:, :, None], axis=1)
        token_mask = jnp.broadcast_to(block_mask[:, None, :, None], (blocks_person, BLOCK, window_span * blocks_person, BLOCK)).reshape(FRAMES, window_rows)
        product = jnp.einsum("qhd,khd->hqk", query_heads, key_heads) * score_scale
        scores = jnp.where(token_mask[None], product, masked_value)
        row_top = jnp.max(scores, axis=-1, keepdims=True)
        row_total = jnp.sum(jnp.where(token_mask[None], jnp.exp(scores - row_top), 0.0), axis=-1, keepdims=True)
        log_total = row_top + jnp.log(row_total)
        probs = jnp.where(token_mask[None], jnp.exp(scores - log_total), 0.0)
        probs_b = lax.optimization_barrier(probs.astype(jnp.bfloat16)).astype(jnp.float32)
        attention = jnp.einsum("hqk,khd->qhd", probs_b, value_heads)
        row_delta = jnp.sum(dout_heads * attention, axis=-1).T
        d_probs = jnp.einsum("qhd,khd->hqk", dout_heads, value_heads)
        d_scores = lax.optimization_barrier((probs * (d_probs - row_delta[:, :, None])).astype(jnp.bfloat16)).astype(jnp.float32)
        query_grad = (jnp.einsum("hqk,khd->qhd", d_scores, key_heads) * score_scale).astype(jnp.bfloat16).reshape(FRAMES, FEATURES)
        key_part = jnp.einsum("hqk,qhd->khd", d_scores, query_heads).reshape(window_rows, FEATURES)
        value_part = jnp.einsum("hqk,qhd->khd", probs_b, dout_heads).reshape(window_rows, FEATURES)
        key_part = lax.optimization_barrier(key_part.astype(jnp.bfloat16)).astype(jnp.float32)
        value_part = lax.optimization_barrier(value_part.astype(jnp.bfloat16)).astype(jnp.float32)
        key_grad = lax.dynamic_update_slice_in_dim(key_grad, lax.dynamic_slice_in_dim(key_grad, start, window_rows, 0) + key_part, start, 0)
        value_grad = lax.dynamic_update_slice_in_dim(value_grad, lax.dynamic_slice_in_dim(value_grad, start, window_rows, 0) + value_part, start, 0)
        return (key_grad, value_grad), query_grad

    empty = jnp.zeros((TOKENS + 2 * margin, FEATURES), jnp.float32)
    (key_grad, value_grad), query_grads = lax.scan(person_step, (empty, empty), jnp.arange(PERSONS, dtype=jnp.int32))
    d_queries = query_grads.reshape(TOKENS, FEATURES)
    d_keys = (key_grad[margin:margin + TOKENS] * score_scale).astype(jnp.bfloat16)
    d_values = value_grad[margin:margin + TOKENS].astype(jnp.bfloat16)
    return (d_queries, d_keys, d_values)
```

```python
import jax
import jax.numpy as jnp
from jax import lax
from jax.experimental import pallas as pl
from jax.experimental.pallas import tpu as pltpu
from jax.sharding import PartitionSpec as P

HEAD_DIM = 64
BLOCK = 64
PERSON = 512
HALF = 256
PAIR = 128
LOCAL = 4
WINDOW = 8
SLOTS = 16
QBLOCKS = 32
MESH = pl.DeviceIdType.MESH


def place():
    ctx = lax.axis_index("ctx")
    head = lax.axis_index("head")
    return ctx, head, lax.rem(ctx, 2), lax.rem(lax.div(ctx, 2), 4), lax.div(ctx, 8)


def chain_peers():
    ctx, head, core, z, group = place()
    order = group * 2 + core

    def at(step):
        spot = order + step
        return (lax.div(spot, 2) * 8 + z * 2 + lax.rem(spot, 2), head)

    return at(-1), at(1), order > 0, order < 15


def greet():
    ctx, head, core, z, group = place()
    barrier = pltpu.get_barrier_semaphore()
    for turn in range(1, 16):
        spot = lax.rem(lax.rem(ctx, 8) + 8 * head + turn, 16)
        pl.semaphore_signal(
            barrier, 1, device_id=(group * 8 + lax.rem(spot, 8), lax.div(spot, 8)), device_id_type=MESH
        )
    before, after, has_before, has_after = chain_peers()

    first, last = (core == 0) & has_before, (core == 1) & has_after

    @pl.when(first)
    def _():
        pl.semaphore_signal(barrier, 1, device_id=before, device_id_type=MESH)

    @pl.when(last)
    def _():
        pl.semaphore_signal(barrier, 1, device_id=after, device_id_type=MESH)

    pl.semaphore_wait(barrier, 15 + jnp.where(first | last, 1, 0))


def remote(src, dst, send, recv, device):
    return pltpu.make_async_remote_copy(
        src_ref=src, dst_ref=dst, send_sem=send, recv_sem=recv, device_id=device, device_id_type=MESH
    )


def compact_lists(blocks_ref, counts_ref, lists_ref):
    ctx, head, core, z, group = place()
    first = (group * 2 + core) * QBLOCKS
    slots = blocks_ref[pl.ds(first, QBLOCKS), :] - (first - 2 * (PERSON // BLOCK))
    row = lax.broadcasted_iota(jnp.int32, (QBLOCKS, 512), 0)
    col = lax.broadcasted_iota(jnp.int32, (QBLOCKS, 512), 1)
    spread = jnp.broadcast_to(counts_ref[...], (QBLOCKS, 512))
    counts = jnp.sum(jnp.where(col == row + first, spread, 0), axis=1, keepdims=True)
    lane = lax.broadcasted_iota(jnp.int32, (QBLOCKS, SLOTS), 1)
    out_lane = lax.broadcasted_iota(jnp.int32, (QBLOCKS, 128), 1)
    total = jnp.zeros((QBLOCKS, 1), jnp.int32)
    lists = jnp.broadcast_to(slots[:, 0:1], (QBLOCKS, 128))
    for slot in range(SLOTS):
        value = slots[:, slot : slot + 1]
        seen = jnp.sum(jnp.where((slots == value) & (lane < slot), 1, 0), axis=1, keepdims=True)
        live = jnp.where((seen == 0) & (counts > slot), 1, 0)
        lists = jnp.where((out_lane == total) & (live > 0), value, lists)
        total = total + live
    lists_ref[...] = jnp.where(out_lane == SLOTS, total, lists)


def exchange_in(
    key_ref, value_ref, query_ref, dout_ref, blocks_ref, counts_ref,
    keys_out, values_out, queries_out, douts_out, lists_ref,
    send_sem, recv_sem, halo_send, halo_recv,
):
    ctx, head, core, z, group = place()
    greet()
    owner_core = lax.div(z, 2)
    person = lax.rem(ctx, 4)
    sources = (key_ref, value_ref, query_ref, dout_ref)
    targets = (keys_out, values_out, queries_out, douts_out)
    bases = (2 * PERSON, 2 * PERSON, 0, 0)

    def piece(which, turn):
        to_z = lax.rem(z + turn % 4, 4)
        to_head = lax.rem(head + turn // 4, 2)
        column = pl.multiple_of((to_head * 4 + to_z) * PAIR, PAIR)
        row = pl.multiple_of(bases[which] + person * PERSON + head * HALF, HALF)
        src = sources[which].at[:, pl.ds(column, PAIR)]
        dst = targets[which].at[pl.ds(row, HALF), :]
        return src, dst, (group * 8 + to_z * 2 + owner_core, to_head)

    order = (6, 2, 5, 7, 4, 1, 3, 0)
    for which in range(4):
        for turn in order:
            src, dst, device = piece(which, turn)
            send, recv = send_sem.at[which, turn], recv_sem.at[which, person, head]
            if turn == 0:

                @pl.when(owner_core == core)
                def _():
                    pltpu.make_async_copy(src, dst, recv).start()

                @pl.when(owner_core != core)
                def _():
                    remote(src, dst, send, recv, device).start()
            else:
                remote(src, dst, send, recv, device).start()
    compact_lists(blocks_ref, counts_ref, lists_ref)
    before, after, has_before, has_after = chain_peers()

    def arrive(which, who):
        for half in range(2):
            rows = pl.ds(bases[which] + who * PERSON + half * HALF, HALF)
            part = targets[which].at[rows, :]
            pltpu.make_async_copy(part, part, recv_sem.at[which, who, half]).wait()

    def halo(which, who):
        target = targets[which]
        src = target.at[pl.ds((2 + who) * PERSON, PERSON), :]
        to = 6 + who if who < 2 else who - 2
        dst = target.at[pl.ds(to * PERSON, PERSON), :]
        return remote(
            src, dst, halo_send.at[which, who], halo_recv.at[which, who], before if who < 2 else after
        )

    for which in range(2):
        for who in range(4):
            arrive(which, who)

            @pl.when(has_before if who < 2 else has_after)
            def _():
                halo(which, who).start()

    for which in range(2, 4):
        for who in range(4):
            arrive(which, who)
    for which in range(2):
        for who in range(4):

            @pl.when(has_before if who < 2 else has_after)
            def _():
                halo(which, who).wait_send()

            @pl.when(has_after if who < 2 else has_before)
            def _():
                halo(which, who).wait_recv()

    for which in range(4):
        for turn in order:
            src, dst, device = piece(which, turn)
            copy = remote(src, dst, send_sem.at[which, turn], recv_sem.at[which, person, head], device)
            if turn == 0:

                @pl.when(owner_core != core)
                def _():
                    copy.wait_send()
            else:
                copy.wait_send()


def attend(
    lists_ref, query_ref, dout_ref, key_ref, value_ref, dquery_ref, dkey_ref, dvalue_ref, dkey_sum, dvalue_sum
):
    rows_all = WINDOW * PERSON

    @pl.loop(0, rows_all // PERSON)
    def _(chunk):
        rows = pl.ds(pl.multiple_of(chunk * PERSON, PERSON), PERSON)
        dkey_sum[rows, :] = jnp.zeros((PERSON, PAIR), jnp.float32)
        dvalue_sum[rows, :] = jnp.zeros((PERSON, PAIR), jnp.float32)

    first_head = lax.broadcasted_iota(jnp.int32, (BLOCK, PAIR), 1) < HEAD_DIM
    scale = HEAD_DIM ** (-0.5)

    def both_heads(block):
        nothing = jnp.zeros_like(block)
        return jnp.concatenate(
            [jnp.where(first_head, block, nothing), jnp.where(first_head, nothing, block)], axis=0
        )

    def body(block, live, width):
        q_rows = pl.ds(pl.multiple_of(block * BLOCK, BLOCK), BLOCK)
        spots = [
            pl.ds(pl.multiple_of(lists_ref[block, slot] * BLOCK, BLOCK), BLOCK) for slot in range(width)
        ]
        queries = both_heads(query_ref[q_rows, :])
        douts = both_heads(dout_ref[q_rows, :])
        keys = jnp.concatenate([key_ref[spot, :] for spot in spots], axis=0)
        values = jnp.concatenate([value_ref[spot, :] for spot in spots], axis=0)
        nt = (((1,), (1,)), ((), ()))
        scores = lax.dot_general(keys, queries, nt, preferred_element_type=jnp.float32) * scale
        fixed = (width - 4) * BLOCK
        tail = lax.broadcasted_iota(jnp.int32, (4 * BLOCK, PAIR), 0) + fixed < live * BLOCK
        tail = jnp.where(tail, scores[fixed:], -1e30)
        scores = jnp.concatenate([scores[:fixed], tail], axis=0) if fixed else tail
        top = jnp.max(scores, axis=0, keepdims=True)
        weights = jnp.exp(scores - top)
        probs = weights * (1.0 / jnp.sum(weights, axis=0, keepdims=True))
        probs_b = probs.astype(jnp.bfloat16)
        d_probs = lax.dot_general(values, douts, nt, preferred_element_type=jnp.float32)
        delta = jnp.sum(probs_b.astype(jnp.float32) * d_probs, axis=0, keepdims=True)
        d_scores = (probs * (d_probs - delta)).astype(jnp.bfloat16)
        d_values = jnp.dot(probs_b, douts, preferred_element_type=jnp.float32)
        d_keys = jnp.dot(d_scores, queries, preferred_element_type=jnp.float32)
        d_queries = lax.dot_general(
            d_scores, keys, (((0,), (0,)), ((), ())), preferred_element_type=jnp.float32
        )
        d_queries = jnp.where(first_head, d_queries[:BLOCK], d_queries[BLOCK:]) * scale
        dquery_ref[q_rows, :] = d_queries.astype(jnp.bfloat16)
        for slot, spot in enumerate(spots):
            part = slice(slot * BLOCK, (slot + 1) * BLOCK)
            dvalue_sum[spot, :] += d_values[part]
            dkey_sum[spot, :] += d_keys[part]

    @pl.loop(0, QBLOCKS)
    def _(block):
        live = lists_ref[block, SLOTS]
        for width in (4, 8, 12, 16):

            @pl.when((live <= width) & (live > width - 4))
            def _():
                body(block, live, width)

    @pl.loop(0, rows_all // PERSON)
    def _(chunk):
        rows = pl.ds(pl.multiple_of(chunk * PERSON, PERSON), PERSON)
        dkey_ref[rows, :] = (dkey_sum[rows, :] * scale).astype(jnp.bfloat16)
        dvalue_ref[rows, :] = dvalue_sum[rows, :].astype(jnp.bfloat16)


def exchange_out(
    dquery_ref, dkey_ref, dvalue_ref,
    dquery_out, dkey_out, dvalue_out,
    arrived, total, send_sem, recv_sem, halo_send, halo_recv,
):
    ctx, head, core, z, group = place()
    greet()
    before, after, has_before, has_after = chain_peers()
    parts = (dkey_ref, dvalue_ref)
    outs = (dquery_out, dkey_out, dvalue_out)

    def halo(which, who):
        spot = 6 + who if who < 2 else who - 2
        return remote(
            parts[which].at[pl.ds(spot * PERSON, PERSON), :],
            arrived.at[which, who],
            halo_send.at[which, who],
            halo_recv.at[which, who],
            after if who < 2 else before,
        )

    for which in range(2):
        for who in range(4):

            @pl.when(has_after if who < 2 else has_before)
            def _():
                halo(which, who).start()

    column = pl.multiple_of((head * 4 + z) * PAIR, PAIR)

    def piece(which, who, half):
        src = dquery_ref if which == 0 else total.at[which - 1]
        src = src.at[pl.ds(who * PERSON + half * HALF, HALF), :]
        dst = outs[which].at[:, pl.ds(column, PAIR)]
        device = (group * 8 + core * 4 + who, jnp.int32(half))
        return src, dst, device

    pair = head * 4 + z

    def send(which, who, half):
        src, dst, device = piece(which, who, half)
        recv = recv_sem.at[which, pair]
        itself = (device[0] == ctx) & (head == half)

        @pl.when(itself)
        def _():
            pltpu.make_async_copy(src, dst, recv).start()

        @pl.when(jnp.logical_not(itself))
        def _():
            remote(src, dst, send_sem.at[which, who, half], recv, device).start()

    for who in range(4):
        for half in range(2):
            send(0, who, half)
    for which in range(2):
        for who in range(4):
            own = parts[which][pl.ds((2 + who) * PERSON, PERSON), :].astype(jnp.float32)
            rows = pl.ds(who * PERSON, PERSON)
            there = has_before if who < 2 else has_after

            @pl.when(there)
            def _():
                halo(which, who).wait_recv()
                total[which, rows, :] = (own + arrived[which, who].astype(jnp.float32)).astype(jnp.bfloat16)

            @pl.when(jnp.logical_not(there))
            def _():
                total[which, rows, :] = own.astype(jnp.bfloat16)

            for half in range(2):
                send(which + 1, who, half)

    for which in range(2):
        for who in range(4):

            @pl.when(has_after if who < 2 else has_before)
            def _():
                halo(which, who).wait_send()

    for which in range(3):
        for who in range(4):
            for half in range(2):
                src, dst, device = piece(which, who, half)
                itself = (device[0] == ctx) & (head == half)

                @pl.when(jnp.logical_not(itself))
                def _():
                    remote(
                        src, dst, send_sem.at[which, who, half], recv_sem.at[which, pair], device
                    ).wait_send()

        for source in range(8):
            part = outs[which].at[:, pl.ds(source * PAIR, PAIR)]
            pltpu.make_async_copy(part, part, recv_sem.at[which, source]).wait()


def on_device(queries, keys_in, values, d_out, pair_blocks, pair_count):
    anywhere = pl.BlockSpec(memory_space=pl.ANY)
    vmem = pl.BlockSpec(memory_space=pltpu.VMEM)
    dma = pltpu.SemaphoreType.DMA
    wide = jax.ShapeDtypeStruct((WINDOW * PERSON, PAIR), jnp.bfloat16)
    narrow = jax.ShapeDtypeStruct((LOCAL * PERSON, PAIR), jnp.bfloat16)
    rows = jax.ShapeDtypeStruct(queries.shape, jnp.bfloat16)
    keys, vals, query, dout, lists = pl.pallas_call(
        exchange_in,
        out_shape=(wide, wide, narrow, narrow, jax.ShapeDtypeStruct((QBLOCKS, 128), jnp.int32)),
        in_specs=[anywhere] * 4 + [vmem] * 2,
        out_specs=(anywhere,) * 4 + (vmem,),
        scratch_shapes=[dma((4, 8)), dma((4, 4, 2)), dma((2, 4)), dma((2, 4))],
        compiler_params=pltpu.CompilerParams(collective_id=0, has_side_effects=True),
        name="exchange_in",
    )(keys_in, values, queries, d_out, pair_blocks, pair_count.reshape(1, -1))
    d_query, d_key, d_value = pl.pallas_call(
        attend,
        out_shape=(narrow, wide, wide),
        in_specs=[pl.BlockSpec(memory_space=pltpu.SMEM)] + [vmem] * 4,
        out_specs=(vmem,) * 3,
        scratch_shapes=[pltpu.VMEM((WINDOW * PERSON, PAIR), jnp.float32)] * 2,
        compiler_params=pltpu.CompilerParams(vmem_limit_bytes=40 << 20),
        name="attend",
    )(lists, query, dout, keys, vals)
    return pl.pallas_call(
        exchange_out,
        out_shape=(rows,) * 3,
        in_specs=[anywhere, vmem, vmem],
        out_specs=(anywhere,) * 3,
        scratch_shapes=[
            pltpu.VMEM((2, 4, PERSON, PAIR), jnp.bfloat16),
            pltpu.VMEM((2, LOCAL * PERSON, PAIR), jnp.bfloat16),
            dma((3, 4, 2)), dma((3, 8)), dma((2, 4)), dma((2, 4)),
        ],
        compiler_params=pltpu.CompilerParams(collective_id=1, has_side_effects=True),
        name="exchange_out",
    )(d_query, d_key, d_value)


def solution(mesh):
    tokens = P(("ctx", "head"), None)
    return jax.shard_map(
        on_device,
        mesh=mesh,
        in_specs=(tokens,) * 4 + (P(), P()),
        out_specs=(tokens,) * 3,
        check_vma=False,
    )
```

```python
import jax
import jax.numpy as jnp
from jax import lax
from jax.experimental import pallas as pl
from jax.experimental.pallas import tpu as pltpu
from jax.sharding import PartitionSpec as P

HEAD_DIM = 64
BLOCK = 64
PERSON = 512
HALF = 256
PAIR = 128
LOCAL = 4
WINDOW = 8
SLOTS = 16
QBLOCKS = 32
LIST_ROWS = 24
STEP = 4
GROUP = 2
MESH = pl.DeviceIdType.MESH


def place():
    ctx = lax.axis_index("ctx")
    head = lax.axis_index("head")
    return ctx, head, lax.rem(ctx, 2), lax.rem(lax.div(ctx, 2), 4), lax.div(ctx, 8)


def chain_peers():
    ctx, head, core, z, group = place()
    order = group * 2 + core

    def at(step):
        spot = order + step
        return (lax.div(spot, 2) * 8 + z * 2 + lax.rem(spot, 2), head)

    return at(-1), at(1), order > 0, order < 15


def greet():
    ctx, head, core, z, group = place()
    barrier = pltpu.get_barrier_semaphore()
    for turn in range(1, 16):
        spot = lax.rem(lax.rem(ctx, 8) + 8 * head + turn, 16)
        pl.semaphore_signal(
            barrier, 1, device_id=(group * 8 + lax.rem(spot, 8), lax.div(spot, 8)), device_id_type=MESH
        )
    before, after, has_before, has_after = chain_peers()

    first, last = (core == 0) & has_before, (core == 1) & has_after

    @pl.when(first)
    def _():
        pl.semaphore_signal(barrier, 1, device_id=before, device_id_type=MESH)

    @pl.when(last)
    def _():
        pl.semaphore_signal(barrier, 1, device_id=after, device_id_type=MESH)

    pl.semaphore_wait(barrier, 15 + jnp.where(first | last, 1, 0))


def remote(src, dst, send, recv, device):
    return pltpu.make_async_remote_copy(
        src_ref=src, dst_ref=dst, send_sem=send, recv_sem=recv, device_id=device, device_id_type=MESH
    )


def compact_lists(blocks_ref, counts_ref, lists_ref):
    ctx, head, core, z, group = place()
    first = (group * 2 + core) * QBLOCKS
    row = lax.broadcasted_iota(jnp.int32, (SLOTS, 512), 0)
    slots = blocks_ref[...] - (first - 2 * (PERSON // BLOCK))
    counts = counts_ref[...]
    out_row = lax.broadcasted_iota(jnp.int32, (LIST_ROWS, 512), 0)
    total = jnp.zeros((1, 512), jnp.int32)
    lists = jnp.broadcast_to(slots[0:1], (LIST_ROWS, 512))
    for slot in range(SLOTS):
        value = slots[slot : slot + 1]
        seen = jnp.sum(jnp.where((slots == value) & (row < slot), 1, 0), axis=0, keepdims=True)
        live = jnp.where((seen == 0) & (counts > slot), 1, 0)
        lists = jnp.where((out_row == total) & (live > 0), value, lists)
        total = total + live
    lists = jnp.where(out_row == SLOTS, total, lists)
    lists = pltpu.roll(lists, lax.rem(512 - first, 512), 1)[:, :128]
    across = lax.broadcasted_iota(jnp.int32, (128, 128), 1)
    down = lax.broadcasted_iota(jnp.int32, (128, 128), 0)
    size = jnp.where(across[0:1] < QBLOCKS, lists[SLOTS : SLOTS + 1], -1)
    size = jnp.broadcast_to(size, (128, 128))
    own = jnp.sum(jnp.where(across == down, size, 0), axis=1, keepdims=True)
    ahead = jnp.where((size > own) | ((size == own) & (across < down)), 1, 0)
    rank = jnp.sum(ahead, axis=1, keepdims=True)
    ranked = jnp.sum(jnp.where(rank == across, down, 0), axis=0, keepdims=True)
    lists_ref[...] = jnp.where(out_row[:, :128] == SLOTS + 1, ranked, lists)


def exchange_in(
    key_ref, value_ref, query_ref, dout_ref, blocks_ref, counts_ref,
    keys_out, values_out, queries_out, douts_out, lists_ref,
    blocks_vmem, counts_vmem, table_sem, send_sem, recv_sem, halo_send, halo_recv,
):
    ctx, head, core, z, group = place()
    tables = [
        pltpu.make_async_copy(blocks_ref, blocks_vmem, table_sem.at[0]),
        pltpu.make_async_copy(counts_ref, counts_vmem, table_sem.at[1]),
    ]
    for table in tables:
        table.start()
    greet()
    owner_core = lax.div(z, 2)
    person = lax.rem(ctx, 4)
    sources = (key_ref, value_ref, query_ref, dout_ref)
    targets = (keys_out, values_out, queries_out, douts_out)
    bases = (2 * PERSON, 2 * PERSON, 0, 0)

    def piece(which, turn):
        to_z = lax.rem(z + turn % 4, 4)
        to_head = lax.rem(head + turn // 4, 2)
        column = pl.multiple_of((to_head * 4 + to_z) * PAIR, PAIR)
        row = pl.multiple_of(bases[which] + person * PERSON + head * HALF, HALF)
        src = sources[which].at[:, pl.ds(column, PAIR)]
        dst = targets[which].at[pl.ds(row, HALF), :]
        return src, dst, (group * 8 + to_z * 2 + owner_core, to_head)

    order = (6, 2, 5, 7, 4, 1, 3, 0)
    for which in range(4):
        for turn in order:
            src, dst, device = piece(which, turn)
            send, recv = send_sem.at[which, turn], recv_sem.at[which, person, head]
            if turn == 0:

                @pl.when(owner_core == core)
                def _():
                    pltpu.make_async_copy(src, dst, recv).start()

                @pl.when(owner_core != core)
                def _():
                    remote(src, dst, send, recv, device).start()
            else:
                remote(src, dst, send, recv, device).start()
    for table in tables:
        table.wait()
    compact_lists(blocks_vmem, counts_vmem, lists_ref)
    before, after, has_before, has_after = chain_peers()

    def arrive(which, who):
        for half in range(2):
            rows = pl.ds(bases[which] + who * PERSON + half * HALF, HALF)
            part = targets[which].at[rows, :]
            pltpu.make_async_copy(part, part, recv_sem.at[which, who, half]).wait()

    def halo(which, who):
        target = targets[which]
        src = target.at[pl.ds((2 + who) * PERSON, PERSON), :]
        to = 6 + who if who < 2 else who - 2
        dst = target.at[pl.ds(to * PERSON, PERSON), :]
        return remote(
            src, dst, halo_send.at[which, who], halo_recv.at[which, who], before if who < 2 else after
        )

    for which in range(2):
        for who in range(4):
            arrive(which, who)

            @pl.when(has_before if who < 2 else has_after)
            def _():
                halo(which, who).start()

    for which in range(2, 4):
        for who in range(4):
            arrive(which, who)
    for which in range(2):
        for who in range(4):

            @pl.when(has_before if who < 2 else has_after)
            def _():
                halo(which, who).wait_send()

            @pl.when(has_after if who < 2 else has_before)
            def _():
                halo(which, who).wait_recv()

    for which in range(4):
        for turn in order:
            src, dst, device = piece(which, turn)
            copy = remote(src, dst, send_sem.at[which, turn], recv_sem.at[which, person, head], device)
            if turn == 0:

                @pl.when(owner_core != core)
                def _():
                    copy.wait_send()
            else:
                copy.wait_send()


def attend(
    lists_ref, query_ref, dout_ref, key_ref, value_ref, dquery_ref, dkey_ref, dvalue_ref, dkey_sum, dvalue_sum
):
    rows_all = WINDOW * PERSON

    @pl.loop(0, rows_all // PERSON)
    def _(chunk):
        rows = pl.ds(pl.multiple_of(chunk * PERSON, PERSON), PERSON)
        dkey_sum[rows, :] = jnp.zeros((PERSON, PAIR), jnp.float32)
        dvalue_sum[rows, :] = jnp.zeros((PERSON, PAIR), jnp.float32)

    first_head = lax.broadcasted_iota(jnp.int32, (BLOCK, PAIR), 1) < HEAD_DIM
    scale = HEAD_DIM ** (-0.5)
    nt = (((1,), (1,)), ((), ()))
    tn = (((0,), (0,)), ((), ()))

    def both_heads(block):
        nothing = jnp.zeros_like(block)
        return [jnp.where(first_head, block, nothing), jnp.where(first_head, nothing, block)]

    def spread(one, two):
        upper = jnp.concatenate(both_heads(one), axis=0)
        lower = jnp.concatenate(both_heads(two), axis=0)
        nothing = jnp.zeros_like(upper)
        return jnp.concatenate(
            [jnp.concatenate([upper, nothing], axis=1), jnp.concatenate([nothing, lower], axis=1)], axis=0
        )

    def load(pair, width):
        blocks = [lists_ref[SLOTS + 1, pair * 2 + i] for i in range(2)]
        lives = [lists_ref[SLOTS, block] for block in blocks]
        q_rows = [pl.ds(pl.multiple_of(block * BLOCK, BLOCK), BLOCK) for block in blocks]
        spots = [
            [pl.ds(pl.multiple_of(lists_ref[slot, block] * BLOCK, BLOCK), BLOCK) for slot in range(width)]
            for block in blocks
        ]
        return lives, q_rows, spots

    def softmax(width, lives, q_rows, spots):
        queries = spread(*[(query_ref[rows, :] * scale).astype(jnp.bfloat16) for rows in q_rows])
        douts = spread(*[dout_ref[rows, :] for rows in q_rows])
        keys = [jnp.concatenate([key_ref[spot, :] for spot in some], axis=0) for some in spots]
        values = [jnp.concatenate([value_ref[spot, :] for spot in some], axis=0) for some in spots]
        both_keys = jnp.concatenate(keys, axis=1)
        both_values = jnp.concatenate(values, axis=1)
        scores = lax.dot_general(both_keys, queries, nt, preferred_element_type=jnp.float32)
        lane = lax.broadcasted_iota(jnp.int32, (1, 2 * PAIR), 1)
        live = jnp.where(lane < PAIR, lives[0], lives[1])
        scores = jnp.concatenate(
            [
                jnp.where(live > slot, scores[slot * BLOCK : (slot + 1) * BLOCK], -1e30)
                for slot in range(width)
            ],
            axis=0,
        )
        top = jnp.max(scores, axis=0, keepdims=True)
        weights = jnp.exp(scores - top)
        d_probs = lax.dot_general(both_values, douts, nt, preferred_element_type=jnp.float32)
        share = 1.0 / jnp.sum(weights, axis=0, keepdims=True)
        delta = jnp.sum(weights * d_probs, axis=0, keepdims=True) * share
        probs = weights * share
        probs_b = probs.astype(jnp.bfloat16)
        d_scores = (probs * (d_probs - delta)).astype(jnp.bfloat16)
        return queries, douts, keys, probs_b, d_scores

    def gradients(q_rows, spots, queries, douts, keys, probs_b, d_scores):
        d_values = jnp.dot(probs_b, douts, preferred_element_type=jnp.float32)
        d_keys = jnp.dot(d_scores, queries, preferred_element_type=jnp.float32)
        for i in range(2):
            lanes = slice(i * PAIR, (i + 1) * PAIR)
            d_queries = lax.dot_general(d_scores[:, lanes], keys[i], tn, preferred_element_type=jnp.float32)
            d_queries = jnp.where(first_head, d_queries[:BLOCK], d_queries[BLOCK:]) * scale
            dquery_ref[q_rows[i], :] = d_queries.astype(jnp.bfloat16)
            for slot, spot in enumerate(spots[i]):
                part = slice(slot * BLOCK, (slot + 1) * BLOCK)
                dvalue_sum[spot, :] += d_values[part, lanes]
                dkey_sum[spot, :] += d_keys[part, lanes]

    def body(group, width):
        loaded = [load(group * GROUP + i, width) for i in range(GROUP)]
        done = [softmax(width, *some) for some in loaded]
        for some, values in zip(loaded, done):
            gradients(*some[1:], *values)

    @pl.loop(0, QBLOCKS // (2 * GROUP))
    def _(group):
        live = lists_ref[SLOTS, lists_ref[SLOTS + 1, group * 2 * GROUP]]
        for width in range(STEP, SLOTS + 1, STEP):

            @pl.when((live <= width) & (live > width - STEP))
            def _():
                body(group, width)

    @pl.loop(0, rows_all // PERSON)
    def _(chunk):
        rows = pl.ds(pl.multiple_of(chunk * PERSON, PERSON), PERSON)
        dkey_ref[rows, :] = dkey_sum[rows, :].astype(jnp.bfloat16)
        dvalue_ref[rows, :] = dvalue_sum[rows, :].astype(jnp.bfloat16)


def exchange_out(
    dquery_ref, dkey_ref, dvalue_ref,
    dquery_out, dkey_out, dvalue_out,
    arrived, total, send_sem, recv_sem, halo_send, halo_recv,
):
    ctx, head, core, z, group = place()
    greet()
    before, after, has_before, has_after = chain_peers()
    parts = (dkey_ref, dvalue_ref)
    outs = (dquery_out, dkey_out, dvalue_out)

    def halo(which, who):
        spot = 6 + who if who < 2 else who - 2
        return remote(
            parts[which].at[pl.ds(spot * PERSON, PERSON), :],
            arrived.at[which, who],
            halo_send.at[which, who],
            halo_recv.at[which, who],
            after if who < 2 else before,
        )

    for which in range(2):
        for who in range(4):

            @pl.when(has_after if who < 2 else has_before)
            def _():
                halo(which, who).start()

    column = pl.multiple_of((head * 4 + z) * PAIR, PAIR)

    def piece(which, who, half):
        src = dquery_ref if which == 0 else total.at[which - 1]
        src = src.at[pl.ds(who * PERSON + half * HALF, HALF), :]
        dst = outs[which].at[:, pl.ds(column, PAIR)]
        device = (group * 8 + core * 4 + who, jnp.int32(half))
        return src, dst, device

    pair = head * 4 + z

    def send(which, who, half):
        src, dst, device = piece(which, who, half)
        recv = recv_sem.at[which, pair]
        itself = (device[0] == ctx) & (head == half)

        @pl.when(itself)
        def _():
            pltpu.make_async_copy(src, dst, recv).start()

        @pl.when(jnp.logical_not(itself))
        def _():
            remote(src, dst, send_sem.at[which, who, half], recv, device).start()

    for who in range(4):
        for half in range(2):
            send(0, who, half)
    for which in range(2):
        for who in range(4):
            own = parts[which][pl.ds((2 + who) * PERSON, PERSON), :].astype(jnp.float32)
            rows = pl.ds(who * PERSON, PERSON)
            there = has_before if who < 2 else has_after

            @pl.when(there)
            def _():
                halo(which, who).wait_recv()
                total[which, rows, :] = (own + arrived[which, who].astype(jnp.float32)).astype(jnp.bfloat16)

            @pl.when(jnp.logical_not(there))
            def _():
                total[which, rows, :] = own.astype(jnp.bfloat16)

            for half in range(2):
                send(which + 1, who, half)

    for which in range(2):
        for who in range(4):

            @pl.when(has_after if who < 2 else has_before)
            def _():
                halo(which, who).wait_send()

    for which in range(3):
        for who in range(4):
            for half in range(2):
                src, dst, device = piece(which, who, half)
                itself = (device[0] == ctx) & (head == half)

                @pl.when(jnp.logical_not(itself))
                def _():
                    remote(
                        src, dst, send_sem.at[which, who, half], recv_sem.at[which, pair], device
                    ).wait_send()

        for source in range(8):
            part = outs[which].at[:, pl.ds(source * PAIR, PAIR)]
            pltpu.make_async_copy(part, part, recv_sem.at[which, source]).wait()


def put_out(dquery_ref, dkey_ref, dvalue_ref, dquery_out, dkey_out, dvalue_out, sem):
    pairs = ((dquery_ref, dquery_out), (dkey_ref, dkey_out), (dvalue_ref, dvalue_out))
    copies = [pltpu.make_async_copy(src, dst, sem.at[i]) for i, (src, dst) in enumerate(pairs)]
    for copy in copies:
        copy.start()
    for copy in copies:
        copy.wait()


def on_device(queries, keys_in, values, d_out, pair_blocks, pair_count):
    hbm = pl.BlockSpec(memory_space=pltpu.HBM)
    vmem = pl.BlockSpec(memory_space=pltpu.VMEM)
    dma = pltpu.SemaphoreType.DMA
    wide = jax.ShapeDtypeStruct((WINDOW * PERSON, PAIR), jnp.bfloat16)
    narrow = jax.ShapeDtypeStruct((LOCAL * PERSON, PAIR), jnp.bfloat16)
    rows = jax.ShapeDtypeStruct(queries.shape, jnp.bfloat16)
    blocks = pair_count.shape[0]
    tables = (pair_blocks.T, pair_count.reshape(1, blocks))
    sources = [
        pltpu.with_memory_space_constraint(x, pltpu.HBM) for x in (keys_in, values, queries, d_out) + tables
    ]
    keys, vals, query, dout, lists = pl.pallas_call(
        exchange_in,
        out_shape=(wide, wide, narrow, narrow, jax.ShapeDtypeStruct((LIST_ROWS, 128), jnp.int32)),
        in_specs=[hbm] * 6,
        out_specs=(vmem,) * 5,
        scratch_shapes=[
            pltpu.VMEM((SLOTS, blocks), jnp.int32),
            pltpu.VMEM((1, blocks), jnp.int32),
            dma((2,)), dma((4, 8)), dma((4, 4, 2)), dma((2, 4)), dma((2, 4)),
        ],
        compiler_params=pltpu.CompilerParams(collective_id=0, has_side_effects=True, vmem_limit_bytes=16 << 20),
        name="exchange_in",
    )(*sources)
    d_query, d_key, d_value = pl.pallas_call(
        attend,
        out_shape=(narrow, wide, wide),
        in_specs=[pl.BlockSpec(memory_space=pltpu.SMEM)] + [vmem] * 4,
        out_specs=(vmem,) * 3,
        scratch_shapes=[pltpu.VMEM((WINDOW * PERSON, PAIR), jnp.float32)] * 2,
        compiler_params=pltpu.CompilerParams(vmem_limit_bytes=24 << 20),
        name="attend",
    )(lists, query, dout, keys, vals)
    results = pl.pallas_call(
        exchange_out,
        out_shape=(rows,) * 3,
        in_specs=[vmem] * 3,
        out_specs=(vmem,) * 3,
        scratch_shapes=[
            pltpu.VMEM((2, 4, PERSON, PAIR), jnp.bfloat16),
            pltpu.VMEM((2, LOCAL * PERSON, PAIR), jnp.bfloat16),
            dma((3, 4, 2)), dma((3, 8)), dma((2, 4)), dma((2, 4)),
        ],
        compiler_params=pltpu.CompilerParams(collective_id=1, has_side_effects=True, vmem_limit_bytes=16 << 20),
        name="exchange_out",
    )(d_query, d_key, d_value)
    return pl.pallas_call(
        put_out,
        out_shape=(rows,) * 3,
        in_specs=[vmem] * 3,
        out_specs=(hbm,) * 3,
        scratch_shapes=[dma((3,))],
        compiler_params=pltpu.CompilerParams(vmem_limit_bytes=8 << 20),
        name="put_out",
    )(*results)


def solution(mesh):
    tokens = P(("ctx", "head"), None)
    return jax.shard_map(
        on_device,
        mesh=mesh,
        in_specs=(tokens,) * 4 + (P(), P()),
        out_specs=(tokens,) * 3,
        check_vma=False,
    )
```

```python
import jax
import jax.numpy as jnp
from jax import lax
from jax.experimental import pallas as pl
from jax.experimental.pallas import tpu as pltpu
from jax.sharding import PartitionSpec as P

HEAD_DIM = 64
BLOCK = 64
PERSON = 512
HALF = 256
PAIR = 128
LOCAL = 4
WINDOW = 8
SLOTS = 16
QBLOCKS = 32
LIST_ROWS = 24
STEP = 4
GROUPS = 8
GROUP = 2
MESH = pl.DeviceIdType.MESH


def place():
    ctx = lax.axis_index("ctx")
    head = lax.axis_index("head")
    return ctx, head, lax.rem(ctx, 2), lax.rem(lax.div(ctx, 2), 4), lax.div(ctx, 8)


def neighbours():
    ctx, head, core, z, group = place()
    far_group = group - 1 + 2 * core
    near = (ctx + 1 - 2 * core, head)
    far = (far_group * 8 + z * 2 + 1 - core, head)
    return near, far, (far_group >= 0) & (far_group < GROUPS), 2 - 2 * core, 2 * core


def on_edge(edge_core):
    ctx, head, core, z, group = place()
    return (core == edge_core) & (group == GROUPS // 2 - edge_core)


def relays(edge_core):
    ctx, head, core, z, group = place()
    return [
        ((k * edge_core + (GROUPS - 1 - k) * (1 - edge_core)) * 8 + z * 2 + 1 - edge_core, head) for k in range(3)
    ]


def relay_role():
    ctx, head, core, z, group = place()
    turn = group * (1 - core) + (GROUPS - 1 - group) * core
    target = ((GROUPS // 2 - core) * 8 + z * 2 + core, head)
    other = ((GROUPS // 2 - 1 + core) * 8 + z * 2 + 1 - core, head)
    return turn < 3, turn + 1, target, other


def greet():
    ctx, head, core, z, group = place()
    barrier = pltpu.get_barrier_semaphore()

    def hello(device):
        pl.semaphore_signal(barrier, 1, device_id=device, device_id_type=MESH)

    for turn in range(1, 16):
        spot = lax.rem(lax.rem(ctx, 8) + 8 * head + turn, 16)
        hello((group * 8 + lax.rem(spot, 8), lax.div(spot, 8)))
    near, far, has_far, near_first, far_first = neighbours()
    edge = on_edge(0) | on_edge(1)
    is_relay, turn, target, other = relay_role()

    @pl.when(has_far)
    def _():
        hello(far)

    @pl.when(is_relay)
    def _():
        hello(other)

    count = 15 + jnp.where(has_far, 1, 0) + jnp.where(edge, 3, 0)
    pl.semaphore_wait(barrier, count)


def far_pieces(source_of, target_of, relay_buf, far_send, far_recv, relay_send, relay_recv):
    ctx, head, core, z, group = place()
    near, far, has_far, near_first, far_first = neighbours()
    edge = on_edge(0) | on_edge(1)
    is_relay, turn, target, other = relay_role()

    def direct(which, q):
        return remote(
            source_of(which, q), target_of(which, q, 1 - core), far_send.at[which, q], far_recv.at[which, q], far
        )

    def round_by(which, q, device):
        return remote(
            source_of(which, q), relay_buf.at[which], far_send.at[which, q], relay_recv.at[which], device
        )

    def onward(which):
        return remote(
            relay_buf.at[which], target_of(which, turn, core), relay_send.at[which], far_recv.at[which, turn], target
        )

    def start(which, q):
        if q == 0:

            @pl.when(has_far)
            def _():
                direct(which, q).start()
        else:

            @pl.when(has_far & jnp.logical_not(edge))
            def _():
                direct(which, q).start()

            for edge_core in range(2):

                @pl.when(on_edge(edge_core))
                def _():
                    round_by(which, q, relays(edge_core)[q - 1]).start()

    def forward(which):
        @pl.when(is_relay)
        def _():
            part = relay_buf.at[which]
            pltpu.make_async_copy(part, part, relay_recv.at[which]).wait()
            onward(which).start()

    def arrived(which, q):
        @pl.when(has_far)
        def _():
            direct(which, q).wait_recv()

    def finish():
        for which in range(2):
            for q in range(4):

                @pl.when(has_far)
                def _():
                    direct(which, q).wait_send()

            @pl.when(is_relay)
            def _():
                onward(which).wait_send()

    return start, forward, arrived, finish


def remote(src, dst, send, recv, device):
    return pltpu.make_async_remote_copy(
        src_ref=src, dst_ref=dst, send_sem=send, recv_sem=recv, device_id=device, device_id_type=MESH
    )


def compact_lists(blocks_ref, counts_ref, lists_ref):
    ctx, head, core, z, group = place()
    first = (group * 2 + core) * QBLOCKS
    row = lax.broadcasted_iota(jnp.int32, (SLOTS, 512), 0)
    slots = blocks_ref[...] - (first - 2 * (PERSON // BLOCK))
    counts = counts_ref[...]
    out_row = lax.broadcasted_iota(jnp.int32, (LIST_ROWS, 512), 0)
    total = jnp.zeros((1, 512), jnp.int32)
    lists = jnp.broadcast_to(slots[0:1], (LIST_ROWS, 512))
    for slot in range(SLOTS):
        value = slots[slot : slot + 1]
        seen = jnp.sum(jnp.where((slots == value) & (row < slot), 1, 0), axis=0, keepdims=True)
        live = jnp.where((seen == 0) & (counts > slot), 1, 0)
        lists = jnp.where((out_row == total) & (live > 0), value, lists)
        total = total + live
    lists = jnp.where(out_row == SLOTS, total, lists)
    lists = pltpu.roll(lists, lax.rem(512 - first, 512), 1)[:, :128]
    across = lax.broadcasted_iota(jnp.int32, (128, 128), 1)
    down = lax.broadcasted_iota(jnp.int32, (128, 128), 0)
    size = jnp.where(across[0:1] < QBLOCKS, lists[SLOTS : SLOTS + 1], -1)
    size = jnp.broadcast_to(size, (128, 128))
    own = jnp.sum(jnp.where(across == down, size, 0), axis=1, keepdims=True)
    ahead = jnp.where((size > own) | ((size == own) & (across < down)), 1, 0)
    rank = jnp.sum(ahead, axis=1, keepdims=True)
    ranked = jnp.sum(jnp.where(rank == across, down, 0), axis=0, keepdims=True)
    lists_ref[...] = jnp.where(out_row[:, :128] == SLOTS + 1, ranked, lists)


def exchange_in(
    key_ref, value_ref, query_ref, dout_ref, blocks_ref, counts_ref,
    keys_out, values_out, queries_out, douts_out, lists_ref,
    blocks_vmem, counts_vmem, table_sem, send_sem, recv_sem, halo_send, halo_recv,
    relay_buf, far_send, far_recv, relay_send, relay_recv,
):
    ctx, head, core, z, group = place()
    tables = [
        pltpu.make_async_copy(blocks_ref, blocks_vmem, table_sem.at[0]),
        pltpu.make_async_copy(counts_ref, counts_vmem, table_sem.at[1]),
    ]
    for table in tables:
        table.start()
    greet()
    owner_core = lax.div(z, 2)
    person = lax.rem(ctx, 4)
    sources = (key_ref, value_ref, query_ref, dout_ref)
    targets = (keys_out, values_out, queries_out, douts_out)
    bases = (2 * PERSON, 2 * PERSON, 0, 0)

    def piece(which, turn):
        to_z = lax.rem(z + turn % 4, 4)
        to_head = lax.rem(head + turn // 4, 2)
        column = pl.multiple_of((to_head * 4 + to_z) * PAIR, PAIR)
        row = pl.multiple_of(bases[which] + person * PERSON + head * HALF, HALF)
        src = sources[which].at[:, pl.ds(column, PAIR)]
        dst = targets[which].at[pl.ds(row, HALF), :]
        return src, dst, (group * 8 + to_z * 2 + owner_core, to_head)

    straight, across = (2, 1, 3, 0), (6, 5, 7, 4)

    def send(which, turn):
        src, dst, device = piece(which, turn)
        out, recv = send_sem.at[which, turn], recv_sem.at[which, person, head]
        if turn == 0:

            @pl.when(owner_core == core)
            def _():
                pltpu.make_async_copy(src, dst, recv).start()

            @pl.when(owner_core != core)
            def _():
                remote(src, dst, out, recv, device).start()
        else:
            remote(src, dst, out, recv, device).start()

    def arrive(which, who):
        for half in range(2):
            rows = pl.ds(pl.multiple_of(bases[which] + who * PERSON + half * HALF, HALF), HALF)
            part = targets[which].at[rows, :]
            pltpu.make_async_copy(part, part, recv_sem.at[which, who, half]).wait()

    near, far, has_far, near_first, far_first = neighbours()

    def halo(which, i):
        src = targets[which].at[pl.ds(pl.multiple_of((2 + near_first + i) * PERSON, PERSON), PERSON), :]
        dst = targets[which].at[pl.ds(pl.multiple_of((6 * core + i) * PERSON, PERSON), PERSON), :]
        return remote(src, dst, halo_send.at[which, i], halo_recv.at[which, i], near)

    def far_source(which, q):
        return targets[which].at[pl.ds(pl.multiple_of((2 + far_first) * PERSON + q * HALF, HALF), HALF), :]

    def far_target(which, q, to_core):
        return targets[which].at[pl.ds(pl.multiple_of(6 * to_core * PERSON + q * HALF, HALF), HALF), :]

    far_start, far_forward, far_arrived, far_finish = far_pieces(
        far_source, far_target, relay_buf, far_send, far_recv, relay_send, relay_recv
    )
    for which in range(3):
        for pair in zip(across, straight):
            for turn in pair:
                send(which, turn)
    for table in tables:
        table.wait()
    compact_lists(blocks_vmem, counts_vmem, lists_ref)
    for which in range(2):
        for i in range(2):
            arrive(which, far_first + i)
            far_start(which, 2 * i)
            far_start(which, 2 * i + 1)
    for pair in zip(across, straight):
        for turn in pair:
            send(3, turn)
    for which in range(2):
        for i in range(2):
            arrive(which, near_first + i)
            halo(which, i).start()
        far_forward(which)
    for which in range(2, 4):
        for who in range(4):
            arrive(which, who)
    for which in range(2):
        for i in range(2):
            halo(which, i).wait_send()
            halo(which, i).wait_recv()
        for q in range(4):
            far_arrived(which, q)
    far_finish()
    for which in range(4):
        for turn in range(8):
            src, dst, device = piece(which, turn)
            copy = remote(src, dst, send_sem.at[which, turn], recv_sem.at[which, person, head], device)
            if turn == 0:

                @pl.when(owner_core != core)
                def _():
                    copy.wait_send()
            else:
                copy.wait_send()


def attend(
    lists_ref, query_ref, dout_ref, key_ref, value_ref, dquery_ref, dkey_ref, dvalue_ref, dkey_sum, dvalue_sum
):
    rows_all = WINDOW * PERSON

    @pl.loop(0, rows_all // PERSON)
    def _(chunk):
        rows = pl.ds(pl.multiple_of(chunk * PERSON, PERSON), PERSON)
        dkey_sum[rows, :] = jnp.zeros((PERSON, PAIR), jnp.float32)
        dvalue_sum[rows, :] = jnp.zeros((PERSON, PAIR), jnp.float32)

    first_head = lax.broadcasted_iota(jnp.int32, (BLOCK, PAIR), 1) < HEAD_DIM
    scale = HEAD_DIM ** (-0.5)
    nt = (((1,), (1,)), ((), ()))
    tn = (((0,), (0,)), ((), ()))

    def both_heads(block):
        nothing = jnp.zeros_like(block)
        return [jnp.where(first_head, block, nothing), jnp.where(first_head, nothing, block)]

    def spread(one, two):
        upper = jnp.concatenate(both_heads(one), axis=0)
        lower = jnp.concatenate(both_heads(two), axis=0)
        nothing = jnp.zeros_like(upper)
        return jnp.concatenate(
            [jnp.concatenate([upper, nothing], axis=1), jnp.concatenate([nothing, lower], axis=1)], axis=0
        )

    def load(pair, width):
        blocks = [lists_ref[SLOTS + 1, pair * 2 + i] for i in range(2)]
        lives = [lists_ref[SLOTS, block] for block in blocks]
        q_rows = [pl.ds(pl.multiple_of(block * BLOCK, BLOCK), BLOCK) for block in blocks]
        spots = [
            [pl.ds(pl.multiple_of(lists_ref[slot, block] * BLOCK, BLOCK), BLOCK) for slot in range(width)]
            for block in blocks
        ]
        return lives, q_rows, spots

    def softmax(width, lives, q_rows, spots):
        queries = spread(*[(query_ref[rows, :] * scale).astype(jnp.bfloat16) for rows in q_rows])
        douts = spread(*[dout_ref[rows, :] for rows in q_rows])
        keys = [jnp.concatenate([key_ref[spot, :] for spot in some], axis=0) for some in spots]
        values = [jnp.concatenate([value_ref[spot, :] for spot in some], axis=0) for some in spots]
        both_keys = jnp.concatenate(keys, axis=1)
        both_values = jnp.concatenate(values, axis=1)
        scores = lax.dot_general(both_keys, queries, nt, preferred_element_type=jnp.float32)
        lane = lax.broadcasted_iota(jnp.int32, (1, 2 * PAIR), 1)
        live = jnp.where(lane < PAIR, lives[0], lives[1])
        scores = jnp.concatenate(
            [
                jnp.where(live > slot, scores[slot * BLOCK : (slot + 1) * BLOCK], -1e30)
                for slot in range(width)
            ],
            axis=0,
        )
        top = jnp.max(scores, axis=0, keepdims=True)
        weights = jnp.exp(scores - top)
        d_probs = lax.dot_general(both_values, douts, nt, preferred_element_type=jnp.float32)
        share = 1.0 / jnp.sum(weights, axis=0, keepdims=True)
        delta = jnp.sum(weights * d_probs, axis=0, keepdims=True) * share
        probs = weights * share
        probs_b = probs.astype(jnp.bfloat16)
        d_scores = (probs * (d_probs - delta)).astype(jnp.bfloat16)
        return queries, douts, keys, probs_b, d_scores

    def gradients(q_rows, spots, queries, douts, keys, probs_b, d_scores):
        d_values = jnp.dot(probs_b, douts, preferred_element_type=jnp.float32)
        d_keys = jnp.dot(d_scores, queries, preferred_element_type=jnp.float32)
        for i in range(2):
            lanes = slice(i * PAIR, (i + 1) * PAIR)
            d_queries = lax.dot_general(d_scores[:, lanes], keys[i], tn, preferred_element_type=jnp.float32)
            d_queries = jnp.where(first_head, d_queries[:BLOCK], d_queries[BLOCK:]) * scale
            dquery_ref[q_rows[i], :] = d_queries.astype(jnp.bfloat16)
            for slot, spot in enumerate(spots[i]):
                part = slice(slot * BLOCK, (slot + 1) * BLOCK)
                dvalue_sum[spot, :] += d_values[part, lanes]
                dkey_sum[spot, :] += d_keys[part, lanes]

    def body(group, width):
        loaded = [load(group * GROUP + i, width) for i in range(GROUP)]
        done = [softmax(width, *some) for some in loaded]
        for some, values in zip(loaded, done):
            gradients(*some[1:], *values)

    @pl.loop(0, QBLOCKS // (2 * GROUP))
    def _(group):
        live = lists_ref[SLOTS, lists_ref[SLOTS + 1, group * 2 * GROUP]]
        for width in range(STEP, SLOTS + 1, STEP):

            @pl.when((live <= width) & (live > width - STEP))
            def _():
                body(group, width)

    @pl.loop(0, rows_all // PERSON)
    def _(chunk):
        rows = pl.ds(pl.multiple_of(chunk * PERSON, PERSON), PERSON)
        dkey_ref[rows, :] = dkey_sum[rows, :].astype(jnp.bfloat16)
        dvalue_ref[rows, :] = dvalue_sum[rows, :].astype(jnp.bfloat16)


def exchange_out(
    dquery_ref, dkey_ref, dvalue_ref,
    dquery_out, dkey_out, dvalue_out,
    arrived, far_arrived_buf, total, send_sem, recv_sem, halo_send, halo_recv,
    relay_buf, far_send, far_recv, relay_send, relay_recv,
):
    ctx, head, core, z, group = place()
    greet()
    near, far, has_far, near_first, far_first = neighbours()
    parts = (dkey_ref, dvalue_ref)
    outs = (dquery_out, dkey_out, dvalue_out)

    def halo(which, i):
        spot = 6 - 6 * core + i
        return remote(
            parts[which].at[pl.ds(pl.multiple_of(spot * PERSON, PERSON), PERSON), :],
            arrived.at[which, i],
            halo_send.at[which, i],
            halo_recv.at[which, i],
            near,
        )

    def far_source(which, q):
        return parts[which].at[pl.ds(pl.multiple_of(6 * core * PERSON + q * HALF, HALF), HALF), :]

    def far_target(which, q, to_core):
        return far_arrived_buf.at[which, pl.ds(pl.multiple_of(q * HALF, HALF), HALF), :]

    far_start, far_forward, far_arrived, far_finish = far_pieces(
        far_source, far_target, relay_buf, far_send, far_recv, relay_send, relay_recv
    )
    for which in range(2):
        for q in range(4):
            far_start(which, q)
    for which in range(2):
        for i in range(2):
            halo(which, i).start()

    pair = head * 4 + z
    column = pl.multiple_of(pair * PAIR, PAIR)

    def piece(which, who, half):
        src = dquery_ref if which == 0 else total.at[which - 1]
        src = src.at[pl.ds(pl.multiple_of(who * PERSON + half * HALF, HALF), HALF), :]
        return src, outs[which].at[:, pl.ds(column, PAIR)], (group * 8 + core * 4 + who, half)

    def send(which, who, half):
        src, dst, device = piece(which, who, half)
        recv = recv_sem.at[which, pair]
        itself = (device[0] == ctx) & (head == half)

        @pl.when(itself)
        def _():
            pltpu.make_async_copy(src, dst, recv).start()

        @pl.when(jnp.logical_not(itself))
        def _():
            remote(src, dst, send_sem.at[which, who, half], recv, device).start()

    def add(which, side, i):
        who = (far_first if side else near_first) + i
        own = parts[which][pl.ds(pl.multiple_of((2 + who) * PERSON, PERSON), PERSON), :].astype(jnp.float32)
        rows = pl.ds(pl.multiple_of(who * PERSON, PERSON), PERSON)
        if not side:
            halo(which, i).wait_recv()
            total[which, rows, :] = (own + arrived[which, i].astype(jnp.float32)).astype(jnp.bfloat16)
            return
        far_arrived(which, 2 * i)
        far_arrived(which, 2 * i + 1)

        @pl.when(has_far)
        def _():
            other = far_arrived_buf[which, pl.ds(i * PERSON, PERSON), :].astype(jnp.float32)
            total[which, rows, :] = (own + other).astype(jnp.bfloat16)

        @pl.when(jnp.logical_not(has_far))
        def _():
            total[which, rows, :] = own.astype(jnp.bfloat16)

    for who in range(4):
        send(0, who, 1 - head)
        send(0, who, head)
    for which in range(2):
        for i in range(2):
            add(which, 0, i)
            send(which + 1, near_first + i, 1 - head)
            send(which + 1, near_first + i, head)
        if which == 0:
            far_forward(0)
            far_forward(1)
    for which in range(2):
        for i in range(2):
            add(which, 1, i)
            send(which + 1, far_first + i, 1 - head)
            send(which + 1, far_first + i, head)
    far_finish()
    for which in range(2):
        for i in range(2):
            halo(which, i).wait_send()

    for which in range(3):
        for who in range(4):
            for half in range(2):
                src, dst, device = piece(which, who, half)

                @pl.when((device[0] != ctx) | (head != half))
                def _():
                    remote(
                        src, dst, send_sem.at[which, who, half], recv_sem.at[which, pair], device
                    ).wait_send()

        for source in range(8):
            part = outs[which].at[:, pl.ds(source * PAIR, PAIR)]
            pltpu.make_async_copy(part, part, recv_sem.at[which, source]).wait()


def put_out(dquery_ref, dkey_ref, dvalue_ref, dquery_out, dkey_out, dvalue_out, sem):
    pairs = ((dquery_ref, dquery_out), (dkey_ref, dkey_out), (dvalue_ref, dvalue_out))
    copies = [pltpu.make_async_copy(src, dst, sem.at[i]) for i, (src, dst) in enumerate(pairs)]
    for copy in copies:
        copy.start()
    for copy in copies:
        copy.wait()


def on_device(queries, keys_in, values, d_out, pair_blocks, pair_count):
    hbm = pl.BlockSpec(memory_space=pltpu.HBM)
    vmem = pl.BlockSpec(memory_space=pltpu.VMEM)
    dma = pltpu.SemaphoreType.DMA
    wide = jax.ShapeDtypeStruct((WINDOW * PERSON, PAIR), jnp.bfloat16)
    narrow = jax.ShapeDtypeStruct((LOCAL * PERSON, PAIR), jnp.bfloat16)
    rows = jax.ShapeDtypeStruct(queries.shape, jnp.bfloat16)
    blocks = pair_count.shape[0]
    tables = (pair_blocks.T, pair_count.reshape(1, blocks))
    sources = [
        pltpu.with_memory_space_constraint(x, pltpu.HBM) for x in (keys_in, values, queries, d_out) + tables
    ]
    keys, vals, query, dout, lists = pl.pallas_call(
        exchange_in,
        out_shape=(wide, wide, narrow, narrow, jax.ShapeDtypeStruct((LIST_ROWS, 128), jnp.int32)),
        in_specs=[hbm] * 6,
        out_specs=(vmem,) * 5,
        scratch_shapes=[
            pltpu.VMEM((SLOTS, blocks), jnp.int32),
            pltpu.VMEM((1, blocks), jnp.int32),
            dma((2,)), dma((4, 8)), dma((4, 4, 2)), dma((2, 2)), dma((2, 2)),
            pltpu.VMEM((2, HALF, PAIR), jnp.bfloat16),
            dma((2, 4)), dma((2, 4)), dma((2,)), dma((2,)),
        ],
        compiler_params=pltpu.CompilerParams(collective_id=0, has_side_effects=True, vmem_limit_bytes=16 << 20),
        name="exchange_in",
    )(*sources)
    d_query, d_key, d_value = pl.pallas_call(
        attend,
        out_shape=(narrow, wide, wide),
        in_specs=[pl.BlockSpec(memory_space=pltpu.SMEM)] + [vmem] * 4,
        out_specs=(vmem,) * 3,
        scratch_shapes=[pltpu.VMEM((WINDOW * PERSON, PAIR), jnp.float32)] * 2,
        compiler_params=pltpu.CompilerParams(vmem_limit_bytes=24 << 20),
        name="attend",
    )(lists, query, dout, keys, vals)
    results = pl.pallas_call(
        exchange_out,
        out_shape=(rows,) * 3,
        in_specs=[vmem] * 3,
        out_specs=(vmem,) * 3,
        scratch_shapes=[
            pltpu.VMEM((2, 2, PERSON, PAIR), jnp.bfloat16),
            pltpu.VMEM((2, 2 * PERSON, PAIR), jnp.bfloat16),
            pltpu.VMEM((2, LOCAL * PERSON, PAIR), jnp.bfloat16),
            dma((3, 4, 2)), dma((3, 8)), dma((2, 2)), dma((2, 2)),
            pltpu.VMEM((2, HALF, PAIR), jnp.bfloat16),
            dma((2, 4)), dma((2, 4)), dma((2,)), dma((2,)),
        ],
        compiler_params=pltpu.CompilerParams(collective_id=1, has_side_effects=True, vmem_limit_bytes=16 << 20),
        name="exchange_out",
    )(d_query, d_key, d_value)
    return pl.pallas_call(
        put_out,
        out_shape=(rows,) * 3,
        in_specs=[vmem] * 3,
        out_specs=(hbm,) * 3,
        scratch_shapes=[dma((3,))],
        compiler_params=pltpu.CompilerParams(vmem_limit_bytes=8 << 20),
        name="put_out",
    )(*results)


def solution(mesh):
    tokens = P(("ctx", "head"), None)
    return jax.shard_map(
        on_device,
        mesh=mesh,
        in_specs=(tokens,) * 4 + (P(), P()),
        out_specs=(tokens,) * 3,
        check_vma=False,
    )
```

```python
import jax
import jax.numpy as jnp
from jax import lax
from jax.experimental import pallas as pl
from jax.experimental.pallas import tpu as pltpu
from jax.sharding import PartitionSpec as P

HEAD_DIM = 64
BLOCK = 64
PERSON = 512
HALF = 256
PAIR = 128
LOCAL = 4
WINDOW = 8
SLOTS = 16
QBLOCKS = 32
LIST_ROWS = 24
STEP = 2
GROUPS = 8
GROUP = 2
MESH = pl.DeviceIdType.MESH


def place():
    ctx = lax.axis_index("ctx")
    head = lax.axis_index("head")
    return ctx, head, lax.rem(ctx, 2), lax.rem(lax.div(ctx, 2), 4), lax.div(ctx, 8)


def neighbours():
    ctx, head, core, z, group = place()
    far_group = group - 1 + 2 * core
    near = (ctx + 1 - 2 * core, head)
    far = (far_group * 8 + z * 2 + 1 - core, head)
    return near, far, (far_group >= 0) & (far_group < GROUPS), 2 - 2 * core, 2 * core


def on_edge(edge_core):
    ctx, head, core, z, group = place()
    return (core == edge_core) & (group == GROUPS // 2 - edge_core)


def relays(edge_core):
    ctx, head, core, z, group = place()
    return [
        ((k * edge_core + (GROUPS - 1 - k) * (1 - edge_core)) * 8 + z * 2 + 1 - edge_core, head) for k in range(3)
    ]


def relay_role():
    ctx, head, core, z, group = place()
    turn = group * (1 - core) + (GROUPS - 1 - group) * core
    target = ((GROUPS // 2 - core) * 8 + z * 2 + core, head)
    other = ((GROUPS // 2 - 1 + core) * 8 + z * 2 + 1 - core, head)
    return turn < 3, turn + 1, target, other


def greet():
    ctx, head, core, z, group = place()
    barrier = pltpu.get_barrier_semaphore()

    def hello(device):
        pl.semaphore_signal(barrier, 1, device_id=device, device_id_type=MESH)

    for turn in range(1, 16):
        spot = lax.rem(lax.rem(ctx, 8) + 8 * head + turn, 16)
        hello((group * 8 + lax.rem(spot, 8), lax.div(spot, 8)))
    near, far, has_far, near_first, far_first = neighbours()
    edge = on_edge(0) | on_edge(1)
    is_relay, turn, target, other = relay_role()

    @pl.when(has_far)
    def _():
        hello(far)

    @pl.when(is_relay)
    def _():
        hello(other)

    count = 15 + jnp.where(has_far, 1, 0) + jnp.where(edge, 3, 0)
    pl.semaphore_wait(barrier, count)


def far_pieces(source_of, target_of, relay_buf, far_send, far_recv, relay_send, relay_recv):
    ctx, head, core, z, group = place()
    near, far, has_far, near_first, far_first = neighbours()
    edge = on_edge(0) | on_edge(1)
    is_relay, turn, target, other = relay_role()

    def direct(which, q):
        return remote(
            source_of(which, q), target_of(which, q, 1 - core), far_send.at[which, q], far_recv.at[which, q], far
        )

    def round_by(which, q, device):
        return remote(
            source_of(which, q), relay_buf.at[which], far_send.at[which, q], relay_recv.at[which], device
        )

    def onward(which):
        return remote(
            relay_buf.at[which], target_of(which, turn, core), relay_send.at[which], far_recv.at[which, turn], target
        )

    def start(which, q):
        if q == 0:

            @pl.when(has_far)
            def _():
                direct(which, q).start()
        else:

            @pl.when(has_far & jnp.logical_not(edge))
            def _():
                direct(which, q).start()

            for edge_core in range(2):

                @pl.when(on_edge(edge_core))
                def _():
                    round_by(which, q, relays(edge_core)[q - 1]).start()

    def forward(which):
        @pl.when(is_relay)
        def _():
            part = relay_buf.at[which]
            pltpu.make_async_copy(part, part, relay_recv.at[which]).wait()
            onward(which).start()

    def arrived(which, q):
        @pl.when(has_far)
        def _():
            direct(which, q).wait_recv()

    def finish():
        for which in range(2):
            for q in range(4):

                @pl.when(has_far)
                def _():
                    direct(which, q).wait_send()

            @pl.when(is_relay)
            def _():
                onward(which).wait_send()

    return start, forward, arrived, finish


def remote(src, dst, send, recv, device):
    return pltpu.make_async_remote_copy(
        src_ref=src, dst_ref=dst, send_sem=send, recv_sem=recv, device_id=device, device_id_type=MESH
    )


def compact_lists(blocks_ref, counts_ref, lists_ref):
    ctx, head, core, z, group = place()
    first = (group * 2 + core) * QBLOCKS
    row = lax.broadcasted_iota(jnp.int32, (SLOTS, 512), 0)
    slots = blocks_ref[...] - (first - 2 * (PERSON // BLOCK))
    counts = counts_ref[...]
    out_row = lax.broadcasted_iota(jnp.int32, (LIST_ROWS, 512), 0)
    total = jnp.zeros((1, 512), jnp.int32)
    lists = jnp.broadcast_to(slots[0:1], (LIST_ROWS, 512))
    for slot in range(SLOTS):
        value = slots[slot : slot + 1]
        seen = jnp.sum(jnp.where((slots == value) & (row < slot), 1, 0), axis=0, keepdims=True)
        live = jnp.where((seen == 0) & (counts > slot), 1, 0)
        lists = jnp.where((out_row == total) & (live > 0), value, lists)
        total = total + live
    lists = jnp.where(out_row == SLOTS, total, lists)
    lists = pltpu.roll(lists, lax.rem(512 - first, 512), 1)[:, :128]
    across = lax.broadcasted_iota(jnp.int32, (128, 128), 1)
    down = lax.broadcasted_iota(jnp.int32, (128, 128), 0)
    size = jnp.where(across[0:1] < QBLOCKS, lists[SLOTS : SLOTS + 1], -1)
    size = jnp.broadcast_to(size, (128, 128))
    own = jnp.sum(jnp.where(across == down, size, 0), axis=1, keepdims=True)
    ahead = jnp.where((size > own) | ((size == own) & (across < down)), 1, 0)
    rank = jnp.sum(ahead, axis=1, keepdims=True)
    ranked = jnp.sum(jnp.where(rank == across, down, 0), axis=0, keepdims=True)
    lists_ref[...] = jnp.where(out_row[:, :128] == SLOTS + 1, ranked, lists)


def exchange_in(
    key_ref, value_ref, query_ref, dout_ref, blocks_ref, counts_ref,
    keys_out, values_out, queries_out, douts_out, lists_ref,
    blocks_vmem, counts_vmem, table_sem, send_sem, recv_sem, halo_send, halo_recv,
    relay_buf, far_send, far_recv, relay_send, relay_recv,
):
    ctx, head, core, z, group = place()
    tables = [
        pltpu.make_async_copy(blocks_ref, blocks_vmem, table_sem.at[0]),
        pltpu.make_async_copy(counts_ref, counts_vmem, table_sem.at[1]),
    ]
    for table in tables:
        table.start()
    greet()
    owner_core = lax.div(z, 2)
    person = lax.rem(ctx, 4)
    sources = (key_ref, value_ref, query_ref, dout_ref)
    targets = (keys_out, values_out, queries_out, douts_out)
    bases = (2 * PERSON, 2 * PERSON, 0, 0)

    def piece(which, turn):
        to_z = lax.rem(z + turn % 4, 4)
        to_head = lax.rem(head + turn // 4, 2)
        column = pl.multiple_of((to_head * 4 + to_z) * PAIR, PAIR)
        row = pl.multiple_of(bases[which] + person * PERSON + head * HALF, HALF)
        src = sources[which].at[:, pl.ds(column, PAIR)]
        dst = targets[which].at[pl.ds(row, HALF), :]
        return src, dst, (group * 8 + to_z * 2 + owner_core, to_head)

    straight, across = (2, 1, 3, 0), (6, 5, 7, 4)

    def send(which, turn):
        src, dst, device = piece(which, turn)
        out, recv = send_sem.at[which, turn], recv_sem.at[which, person, head]
        if turn == 0:

            @pl.when(owner_core == core)
            def _():
                pltpu.make_async_copy(src, dst, recv).start()

            @pl.when(owner_core != core)
            def _():
                remote(src, dst, out, recv, device).start()
        else:
            remote(src, dst, out, recv, device).start()

    def arrive(which, who):
        for half in range(2):
            rows = pl.ds(pl.multiple_of(bases[which] + who * PERSON + half * HALF, HALF), HALF)
            part = targets[which].at[rows, :]
            pltpu.make_async_copy(part, part, recv_sem.at[which, who, half]).wait()

    near, far, has_far, near_first, far_first = neighbours()

    def halo(which, i):
        src = targets[which].at[pl.ds(pl.multiple_of((2 + near_first + i) * PERSON, PERSON), PERSON), :]
        dst = targets[which].at[pl.ds(pl.multiple_of((6 * core + i) * PERSON, PERSON), PERSON), :]
        return remote(src, dst, halo_send.at[which, i], halo_recv.at[which, i], near)

    def far_source(which, q):
        return targets[which].at[pl.ds(pl.multiple_of((2 + far_first) * PERSON + q * HALF, HALF), HALF), :]

    def far_target(which, q, to_core):
        return targets[which].at[pl.ds(pl.multiple_of(6 * to_core * PERSON + q * HALF, HALF), HALF), :]

    far_start, far_forward, far_arrived, far_finish = far_pieces(
        far_source, far_target, relay_buf, far_send, far_recv, relay_send, relay_recv
    )
    for which in range(3):
        for pair in zip(across, straight):
            for turn in pair:
                send(which, turn)
    for table in tables:
        table.wait()
    compact_lists(blocks_vmem, counts_vmem, lists_ref)
    for which in range(2):
        for i in range(2):
            arrive(which, far_first + i)
            far_start(which, 2 * i)
            far_start(which, 2 * i + 1)
    passes_on = relay_role()[0]

    @pl.when(jnp.logical_not(passes_on))
    def _():
        for pair in zip(across, straight):
            for turn in pair:
                send(3, turn)

    @pl.when(passes_on)
    def _():
        for turn in straight:
            send(3, turn)

    for which in range(2):
        for i in range(2):
            arrive(which, near_first + i)
            halo(which, i).start()
        far_forward(which)

    @pl.when(passes_on)
    def _():
        for turn in across:
            send(3, turn)

    for which in range(2, 4):
        for who in range(4):
            arrive(which, who)
    for which in range(2):
        for i in range(2):
            halo(which, i).wait_send()
            halo(which, i).wait_recv()
        for q in range(4):
            far_arrived(which, q)
    far_finish()
    for which in range(4):
        for turn in range(8):
            src, dst, device = piece(which, turn)
            copy = remote(src, dst, send_sem.at[which, turn], recv_sem.at[which, person, head], device)
            if turn == 0:

                @pl.when(owner_core != core)
                def _():
                    copy.wait_send()
            else:
                copy.wait_send()


def attend(
    lists_ref, query_ref, dout_ref, key_ref, value_ref, dquery_ref, dkey_ref, dvalue_ref, dkey_sum, dvalue_sum
):
    rows_all = WINDOW * PERSON

    @pl.loop(0, rows_all // PERSON)
    def _(chunk):
        rows = pl.ds(pl.multiple_of(chunk * PERSON, PERSON), PERSON)
        dkey_sum[rows, :] = jnp.zeros((PERSON, PAIR), jnp.float32)
        dvalue_sum[rows, :] = jnp.zeros((PERSON, PAIR), jnp.float32)

    first_head = lax.broadcasted_iota(jnp.int32, (BLOCK, PAIR), 1) < HEAD_DIM
    scale = HEAD_DIM ** (-0.5)
    nt = (((1,), (1,)), ((), ()))
    tn = (((0,), (0,)), ((), ()))

    def both_heads(block):
        nothing = jnp.zeros_like(block)
        return [jnp.where(first_head, block, nothing), jnp.where(first_head, nothing, block)]

    def spread(one, two):
        upper = jnp.concatenate(both_heads(one), axis=0)
        lower = jnp.concatenate(both_heads(two), axis=0)
        nothing = jnp.zeros_like(upper)
        return jnp.concatenate(
            [jnp.concatenate([upper, nothing], axis=1), jnp.concatenate([nothing, lower], axis=1)], axis=0
        )

    def load(pair, width):
        blocks = [lists_ref[SLOTS + 1, pair * 2 + i] for i in range(2)]
        lives = [lists_ref[SLOTS, block] for block in blocks]
        q_rows = [pl.ds(pl.multiple_of(block * BLOCK, BLOCK), BLOCK) for block in blocks]
        spots = [
            [pl.ds(pl.multiple_of(lists_ref[slot, block] * BLOCK, BLOCK), BLOCK) for slot in range(width)]
            for block in blocks
        ]
        return lives, q_rows, spots

    def softmax(width, lives, q_rows, spots):
        queries = spread(*[(query_ref[rows, :] * scale).astype(jnp.bfloat16) for rows in q_rows])
        douts = spread(*[dout_ref[rows, :] for rows in q_rows])
        keys = [jnp.concatenate([key_ref[spot, :] for spot in some], axis=0) for some in spots]
        values = [jnp.concatenate([value_ref[spot, :] for spot in some], axis=0) for some in spots]
        both_keys = jnp.concatenate(keys, axis=1)
        both_values = jnp.concatenate(values, axis=1)
        scores = lax.dot_general(both_keys, queries, nt, preferred_element_type=jnp.float32)
        lane = lax.broadcasted_iota(jnp.int32, (1, 2 * PAIR), 1)
        live = jnp.where(lane < PAIR, lives[0], lives[1])
        scores = jnp.concatenate(
            [
                jnp.where(live > slot, scores[slot * BLOCK : (slot + 1) * BLOCK], -1e30)
                for slot in range(width)
            ],
            axis=0,
        )
        top = jnp.max(scores, axis=0, keepdims=True)
        weights = jnp.exp(scores - top)
        d_probs = lax.dot_general(both_values, douts, nt, preferred_element_type=jnp.float32)
        share = 1.0 / jnp.sum(weights, axis=0, keepdims=True)
        delta = jnp.sum(weights * d_probs, axis=0, keepdims=True) * share
        probs = weights * share
        probs_b = probs.astype(jnp.bfloat16)
        d_scores = (probs * (d_probs - delta)).astype(jnp.bfloat16)
        return queries, douts, keys, probs_b, d_scores

    def gradients(q_rows, spots, queries, douts, keys, probs_b, d_scores):
        d_values = jnp.dot(probs_b, douts, preferred_element_type=jnp.float32)
        d_keys = jnp.dot(d_scores, queries, preferred_element_type=jnp.float32)
        for i in range(2):
            lanes = slice(i * PAIR, (i + 1) * PAIR)
            d_queries = lax.dot_general(d_scores[:, lanes], keys[i], tn, preferred_element_type=jnp.float32)
            d_queries = jnp.where(first_head, d_queries[:BLOCK], d_queries[BLOCK:]) * scale
            dquery_ref[q_rows[i], :] = d_queries.astype(jnp.bfloat16)
            for slot, spot in enumerate(spots[i]):
                part = slice(slot * BLOCK, (slot + 1) * BLOCK)
                dvalue_sum[spot, :] += d_values[part, lanes]
                dkey_sum[spot, :] += d_keys[part, lanes]

    def body(group, width):
        loaded = [load(group * GROUP + i, width) for i in range(GROUP)]
        done = [softmax(width, *some) for some in loaded]
        for some, values in zip(loaded, done):
            gradients(*some[1:], *values)

    @pl.loop(0, QBLOCKS // (2 * GROUP))
    def _(group):
        live = lists_ref[SLOTS, lists_ref[SLOTS + 1, group * 2 * GROUP]]
        for width in range(STEP, SLOTS + 1, STEP):

            @pl.when((live <= width) & (live > width - STEP))
            def _():
                body(group, width)

    @pl.loop(0, rows_all // PERSON)
    def _(chunk):
        rows = pl.ds(pl.multiple_of(chunk * PERSON, PERSON), PERSON)
        dkey_ref[rows, :] = dkey_sum[rows, :].astype(jnp.bfloat16)
        dvalue_ref[rows, :] = dvalue_sum[rows, :].astype(jnp.bfloat16)


def exchange_out(
    dquery_ref, dkey_ref, dvalue_ref,
    dquery_out, dkey_out, dvalue_out,
    arrived, far_arrived_buf, total, send_sem, recv_sem, halo_send, halo_recv,
    relay_buf, far_send, far_recv, relay_send, relay_recv,
):
    ctx, head, core, z, group = place()
    greet()
    near, far, has_far, near_first, far_first = neighbours()
    parts = (dkey_ref, dvalue_ref)
    outs = (dquery_out, dkey_out, dvalue_out)

    def halo(which, i):
        spot = 6 - 6 * core + i
        return remote(
            parts[which].at[pl.ds(pl.multiple_of(spot * PERSON, PERSON), PERSON), :],
            arrived.at[which, i],
            halo_send.at[which, i],
            halo_recv.at[which, i],
            near,
        )

    def far_source(which, q):
        return parts[which].at[pl.ds(pl.multiple_of(6 * core * PERSON + q * HALF, HALF), HALF), :]

    def far_target(which, q, to_core):
        return far_arrived_buf.at[which, pl.ds(pl.multiple_of(q * HALF, HALF), HALF), :]

    far_start, far_forward, far_arrived, far_finish = far_pieces(
        far_source, far_target, relay_buf, far_send, far_recv, relay_send, relay_recv
    )
    for which in range(2):
        for q in range(4):
            far_start(which, q)
    for which in range(2):
        for i in range(2):
            halo(which, i).start()

    pair = head * 4 + z
    column = pl.multiple_of(pair * PAIR, PAIR)

    def piece(which, who, half):
        src = dquery_ref if which == 0 else total.at[which - 1]
        src = src.at[pl.ds(pl.multiple_of(who * PERSON + half * HALF, HALF), HALF), :]
        return src, outs[which].at[:, pl.ds(column, PAIR)], (group * 8 + core * 4 + who, half)

    def send(which, who, half):
        src, dst, device = piece(which, who, half)
        recv = recv_sem.at[which, pair]
        itself = (device[0] == ctx) & (head == half)

        @pl.when(itself)
        def _():
            pltpu.make_async_copy(src, dst, recv).start()

        @pl.when(jnp.logical_not(itself))
        def _():
            remote(src, dst, send_sem.at[which, who, half], recv, device).start()

    def add(which, side, i):
        who = (far_first if side else near_first) + i
        own = parts[which][pl.ds(pl.multiple_of((2 + who) * PERSON, PERSON), PERSON), :].astype(jnp.float32)
        rows = pl.ds(pl.multiple_of(who * PERSON, PERSON), PERSON)
        if not side:
            halo(which, i).wait_recv()
            total[which, rows, :] = (own + arrived[which, i].astype(jnp.float32)).astype(jnp.bfloat16)
            return
        far_arrived(which, 2 * i)
        far_arrived(which, 2 * i + 1)

        @pl.when(has_far)
        def _():
            other = far_arrived_buf[which, pl.ds(i * PERSON, PERSON), :].astype(jnp.float32)
            total[which, rows, :] = (own + other).astype(jnp.bfloat16)

        @pl.when(jnp.logical_not(has_far))
        def _():
            total[which, rows, :] = own.astype(jnp.bfloat16)

    passes_on = relay_role()[0]

    def key_across():
        for i in range(2):
            send(1, near_first + i, 1 - head)

    for who in range(4):
        send(0, who, 1 - head)
        send(0, who, head)
    for i in range(2):
        add(0, 0, i)
        send(1, near_first + i, head)
    pl.when(jnp.logical_not(passes_on))(key_across)
    for which in range(2):
        far_forward(which)
    pl.when(passes_on)(key_across)
    for i in range(2):
        add(1, 0, i)
        send(2, near_first + i, 1 - head)
        send(2, near_first + i, head)
    for which in range(2):
        for i in range(2):
            add(which, 1, i)
            send(which + 1, far_first + i, 1 - head)
            send(which + 1, far_first + i, head)
    far_finish()
    for which in range(2):
        for i in range(2):
            halo(which, i).wait_send()

    for which in range(3):
        for who in range(4):
            for half in range(2):
                src, dst, device = piece(which, who, half)

                @pl.when((device[0] != ctx) | (head != half))
                def _():
                    remote(
                        src, dst, send_sem.at[which, who, half], recv_sem.at[which, pair], device
                    ).wait_send()

        for source in range(8):
            part = outs[which].at[:, pl.ds(source * PAIR, PAIR)]
            pltpu.make_async_copy(part, part, recv_sem.at[which, source]).wait()


def put_out(dquery_ref, dkey_ref, dvalue_ref, dquery_out, dkey_out, dvalue_out, sem):
    pairs = ((dquery_ref, dquery_out), (dkey_ref, dkey_out), (dvalue_ref, dvalue_out))
    copies = [pltpu.make_async_copy(src, dst, sem.at[i]) for i, (src, dst) in enumerate(pairs)]
    for copy in copies:
        copy.start()
    for copy in copies:
        copy.wait()


def on_device(queries, keys_in, values, d_out, pair_blocks, pair_count):
    hbm = pl.BlockSpec(memory_space=pltpu.HBM)
    vmem = pl.BlockSpec(memory_space=pltpu.VMEM)
    dma = pltpu.SemaphoreType.DMA
    wide = jax.ShapeDtypeStruct((WINDOW * PERSON, PAIR), jnp.bfloat16)
    narrow = jax.ShapeDtypeStruct((LOCAL * PERSON, PAIR), jnp.bfloat16)
    rows = jax.ShapeDtypeStruct(queries.shape, jnp.bfloat16)
    blocks = pair_count.shape[0]
    tables = (pair_blocks.T, pair_count.reshape(1, blocks))
    sources = [
        pltpu.with_memory_space_constraint(x, pltpu.HBM) for x in (keys_in, values, queries, d_out) + tables
    ]
    keys, vals, query, dout, lists = pl.pallas_call(
        exchange_in,
        out_shape=(wide, wide, narrow, narrow, jax.ShapeDtypeStruct((LIST_ROWS, 128), jnp.int32)),
        in_specs=[hbm] * 6,
        out_specs=(vmem,) * 5,
        scratch_shapes=[
            pltpu.VMEM((SLOTS, blocks), jnp.int32),
            pltpu.VMEM((1, blocks), jnp.int32),
            dma((2,)), dma((4, 8)), dma((4, 4, 2)), dma((2, 2)), dma((2, 2)),
            pltpu.VMEM((2, HALF, PAIR), jnp.bfloat16),
            dma((2, 4)), dma((2, 4)), dma((2,)), dma((2,)),
        ],
        compiler_params=pltpu.CompilerParams(collective_id=0, has_side_effects=True, vmem_limit_bytes=16 << 20),
        name="exchange_in",
    )(*sources)
    d_query, d_key, d_value = pl.pallas_call(
        attend,
        out_shape=(narrow, wide, wide),
        in_specs=[pl.BlockSpec(memory_space=pltpu.SMEM)] + [vmem] * 4,
        out_specs=(vmem,) * 3,
        scratch_shapes=[pltpu.VMEM((WINDOW * PERSON, PAIR), jnp.float32)] * 2,
        compiler_params=pltpu.CompilerParams(vmem_limit_bytes=24 << 20),
        name="attend",
    )(lists, query, dout, keys, vals)
    results = pl.pallas_call(
        exchange_out,
        out_shape=(rows,) * 3,
        in_specs=[vmem] * 3,
        out_specs=(vmem,) * 3,
        scratch_shapes=[
            pltpu.VMEM((2, 2, PERSON, PAIR), jnp.bfloat16),
            pltpu.VMEM((2, 2 * PERSON, PAIR), jnp.bfloat16),
            pltpu.VMEM((2, LOCAL * PERSON, PAIR), jnp.bfloat16),
            dma((3, 4, 2)), dma((3, 8)), dma((2, 2)), dma((2, 2)),
            pltpu.VMEM((2, HALF, PAIR), jnp.bfloat16),
            dma((2, 4)), dma((2, 4)), dma((2,)), dma((2,)),
        ],
        compiler_params=pltpu.CompilerParams(collective_id=1, has_side_effects=True, vmem_limit_bytes=16 << 20),
        name="exchange_out",
    )(d_query, d_key, d_value)
    return pl.pallas_call(
        put_out,
        out_shape=(rows,) * 3,
        in_specs=[vmem] * 3,
        out_specs=(hbm,) * 3,
        scratch_shapes=[dma((3,))],
        compiler_params=pltpu.CompilerParams(vmem_limit_bytes=8 << 20),
        name="put_out",
    )(*results)


def solution(mesh):
    tokens = P(("ctx", "head"), None)
    return jax.shard_map(
        on_device,
        mesh=mesh,
        in_specs=(tokens,) * 4 + (P(), P()),
        out_specs=(tokens,) * 3,
        check_vma=False,
    )
```

```python
import jax
import jax.numpy as jnp
from jax import lax
from jax.experimental import pallas as pl
from jax.experimental.pallas import tpu as pltpu
from jax.sharding import PartitionSpec as P

HEAD_DIM = 64
BLOCK = 64
PERSON = 512
HALF = 256
PAIR = 128
LOCAL = 4
WINDOW = 8
SLOTS = 16
QBLOCKS = 32
LIST_ROWS = 24
STEP = 2
GROUPS = 8
GROUP = 2
MESH = pl.DeviceIdType.MESH


def place():
    ctx = lax.axis_index("ctx")
    head = lax.axis_index("head")
    return ctx, head, lax.rem(ctx, 2), lax.rem(lax.div(ctx, 2), 4), lax.div(ctx, 8)


def neighbours():
    ctx, head, core, z, group = place()
    far_group = group - 1 + 2 * core
    near = (ctx + 1 - 2 * core, head)
    far = (far_group * 8 + z * 2 + 1 - core, head)
    return near, far, (far_group >= 0) & (far_group < GROUPS), 2 - 2 * core, 2 * core


def on_edge(edge_core):
    ctx, head, core, z, group = place()
    return (core == edge_core) & (group == GROUPS // 2 - edge_core)


def relays(edge_core):
    ctx, head, core, z, group = place()
    return [
        ((k * edge_core + (GROUPS - 1 - k) * (1 - edge_core)) * 8 + z * 2 + 1 - edge_core, head) for k in range(3)
    ]


def relay_role():
    ctx, head, core, z, group = place()
    turn = group * (1 - core) + (GROUPS - 1 - group) * core
    target = ((GROUPS // 2 - core) * 8 + z * 2 + core, head)
    other = ((GROUPS // 2 - 1 + core) * 8 + z * 2 + 1 - core, head)
    return turn < 3, turn + 1, target, other


def greet(meanwhile=None):
    ctx, head, core, z, group = place()
    barrier = pltpu.get_barrier_semaphore()

    def hello(device):
        pl.semaphore_signal(barrier, 1, device_id=device, device_id_type=MESH)

    for turn in range(1, 16):
        spot = lax.rem(lax.rem(ctx, 8) + 8 * head + turn, 16)
        hello((group * 8 + lax.rem(spot, 8), lax.div(spot, 8)))
    near, far, has_far, near_first, far_first = neighbours()
    edge = on_edge(0) | on_edge(1)
    is_relay, turn, target, other = relay_role()

    @pl.when(has_far)
    def _():
        hello(far)

    @pl.when(is_relay)
    def _():
        hello(other)

    if meanwhile is not None:
        meanwhile()
    count = 15 + jnp.where(has_far, 1, 0) + jnp.where(edge, 3, 0)
    pl.semaphore_wait(barrier, count)


def far_pieces(source_of, target_of, relay_buf, far_send, far_recv, relay_send, relay_recv):
    ctx, head, core, z, group = place()
    near, far, has_far, near_first, far_first = neighbours()
    edge = on_edge(0) | on_edge(1)
    is_relay, turn, target, other = relay_role()

    def direct(which, q):
        return remote(
            source_of(which, q), target_of(which, q, 1 - core), far_send.at[which, q], far_recv.at[which, q], far
        )

    def round_by(which, q, device):
        return remote(
            source_of(which, q), relay_buf.at[which], far_send.at[which, q], relay_recv.at[which], device
        )

    def onward(which):
        return remote(
            relay_buf.at[which], target_of(which, turn, core), relay_send.at[which], far_recv.at[which, turn], target
        )

    def start(which, q):
        if q == 0:

            @pl.when(has_far)
            def _():
                direct(which, q).start()
        else:

            @pl.when(has_far & jnp.logical_not(edge))
            def _():
                direct(which, q).start()

            for edge_core in range(2):

                @pl.when(on_edge(edge_core))
                def _():
                    round_by(which, q, relays(edge_core)[q - 1]).start()

    def forward(which):
        @pl.when(is_relay)
        def _():
            part = relay_buf.at[which]
            pltpu.make_async_copy(part, part, relay_recv.at[which]).wait()
            onward(which).start()

    def arrived(which, q):
        @pl.when(has_far)
        def _():
            direct(which, q).wait_recv()

    def finish():
        for which in range(2):
            for q in range(4):

                @pl.when(has_far)
                def _():
                    direct(which, q).wait_send()

            @pl.when(is_relay)
            def _():
                onward(which).wait_send()

    return start, forward, arrived, finish


def remote(src, dst, send, recv, device):
    return pltpu.make_async_remote_copy(
        src_ref=src, dst_ref=dst, send_sem=send, recv_sem=recv, device_id=device, device_id_type=MESH
    )


def compact_lists(blocks_ref, counts_ref, lists_ref):
    ctx, head, core, z, group = place()
    first = (group * 2 + core) * QBLOCKS
    row = lax.broadcasted_iota(jnp.int32, (SLOTS, 512), 0)
    slots = blocks_ref[...] - (first - 2 * (PERSON // BLOCK))
    counts = counts_ref[...]
    out_row = lax.broadcasted_iota(jnp.int32, (LIST_ROWS, 512), 0)
    total = jnp.zeros((1, 512), jnp.int32)
    lists = jnp.broadcast_to(slots[0:1], (LIST_ROWS, 512))
    for slot in range(SLOTS):
        value = slots[slot : slot + 1]
        seen = jnp.sum(jnp.where((slots == value) & (row < slot), 1, 0), axis=0, keepdims=True)
        live = jnp.where((seen == 0) & (counts > slot), 1, 0)
        lists = jnp.where((out_row == total) & (live > 0), value, lists)
        total = total + live
    lists = jnp.where(out_row == SLOTS, total, lists)
    lists = pltpu.roll(lists, lax.rem(512 - first, 512), 1)[:, :128]
    across = lax.broadcasted_iota(jnp.int32, (128, 128), 1)
    down = lax.broadcasted_iota(jnp.int32, (128, 128), 0)
    size = jnp.where(across[0:1] < QBLOCKS, lists[SLOTS : SLOTS + 1], -1)
    size = jnp.broadcast_to(size, (128, 128))
    own = jnp.sum(jnp.where(across == down, size, 0), axis=1, keepdims=True)
    ahead = jnp.where((size > own) | ((size == own) & (across < down)), 1, 0)
    rank = jnp.sum(ahead, axis=1, keepdims=True)
    ranked = jnp.sum(jnp.where(rank == across, down, 0), axis=0, keepdims=True)
    lists_ref[...] = jnp.where(out_row[:, :128] == SLOTS + 1, ranked, lists)


def exchange_in(
    key_ref, value_ref, query_ref, dout_ref, blocks_ref, counts_ref,
    keys_out, values_out, queries_out, douts_out, lists_ref, dkey_zero, dvalue_zero,
    blocks_vmem, counts_vmem, table_sem, send_sem, recv_sem, halo_send, halo_recv,
    relay_buf, far_send, far_recv, relay_send, relay_recv,
):
    ctx, head, core, z, group = place()
    tables = [
        pltpu.make_async_copy(blocks_ref, blocks_vmem, table_sem.at[0]),
        pltpu.make_async_copy(counts_ref, counts_vmem, table_sem.at[1]),
    ]
    for table in tables:
        table.start()
    greet()
    owner_core = lax.div(z, 2)
    person = lax.rem(ctx, 4)
    sources = (key_ref, value_ref, query_ref, dout_ref)
    targets = (keys_out, values_out, queries_out, douts_out)
    bases = (2 * PERSON, 2 * PERSON, 0, 0)

    def piece(which, turn):
        to_z = lax.rem(z + turn % 4, 4)
        to_head = lax.rem(head + turn // 4, 2)
        column = pl.multiple_of((to_head * 4 + to_z) * PAIR, PAIR)
        row = pl.multiple_of(bases[which] + person * PERSON + head * HALF, HALF)
        src = sources[which].at[:, pl.ds(column, PAIR)]
        dst = targets[which].at[pl.ds(row, HALF), :]
        return src, dst, (group * 8 + to_z * 2 + owner_core, to_head)

    straight, across = (2, 1, 3, 0), (6, 5, 7, 4)

    def send(which, turn):
        src, dst, device = piece(which, turn)
        out, recv = send_sem.at[which, turn], recv_sem.at[which, person, head]
        if turn == 0:

            @pl.when(owner_core == core)
            def _():
                pltpu.make_async_copy(src, dst, recv).start()

            @pl.when(owner_core != core)
            def _():
                remote(src, dst, out, recv, device).start()
        else:
            remote(src, dst, out, recv, device).start()

    def arrive(which, who):
        for half in range(2):
            rows = pl.ds(pl.multiple_of(bases[which] + who * PERSON + half * HALF, HALF), HALF)
            part = targets[which].at[rows, :]
            pltpu.make_async_copy(part, part, recv_sem.at[which, who, half]).wait()

    near, far, has_far, near_first, far_first = neighbours()

    def halo(which, i):
        src = targets[which].at[pl.ds(pl.multiple_of((2 + near_first + i) * PERSON, PERSON), PERSON), :]
        dst = targets[which].at[pl.ds(pl.multiple_of((6 * core + i) * PERSON, PERSON), PERSON), :]
        return remote(src, dst, halo_send.at[which, i], halo_recv.at[which, i], near)

    def far_source(which, q):
        return targets[which].at[pl.ds(pl.multiple_of((2 + far_first) * PERSON + q * HALF, HALF), HALF), :]

    def far_target(which, q, to_core):
        return targets[which].at[pl.ds(pl.multiple_of(6 * to_core * PERSON + q * HALF, HALF), HALF), :]

    far_start, far_forward, far_arrived, far_finish = far_pieces(
        far_source, far_target, relay_buf, far_send, far_recv, relay_send, relay_recv
    )
    for which in range(3):
        for pair in zip(across, straight):
            for turn in pair:
                send(which, turn)
    for table in tables:
        table.wait()
    compact_lists(blocks_vmem, counts_vmem, lists_ref)

    @pl.loop(0, WINDOW)
    def _(chunk):
        rows = pl.ds(pl.multiple_of(chunk * PERSON, PERSON), PERSON)
        dkey_zero[rows, :] = jnp.zeros((PERSON, PAIR), jnp.float32)
        dvalue_zero[rows, :] = jnp.zeros((PERSON, PAIR), jnp.float32)

    for which in range(2):
        for i in range(2):
            arrive(which, far_first + i)
            far_start(which, 2 * i)
            far_start(which, 2 * i + 1)
    passes_on = relay_role()[0]

    @pl.when(jnp.logical_not(passes_on))
    def _():
        for pair in zip(across, straight):
            for turn in pair:
                send(3, turn)

    @pl.when(passes_on)
    def _():
        for turn in straight:
            send(3, turn)

    for which in range(2):
        for i in range(2):
            arrive(which, near_first + i)
            halo(which, i).start()
        far_forward(which)

    @pl.when(passes_on)
    def _():
        for turn in across:
            send(3, turn)

    for which in range(2, 4):
        for who in range(4):
            arrive(which, who)
    for which in range(2):
        for i in range(2):
            halo(which, i).wait_send()
            halo(which, i).wait_recv()
        for q in range(4):
            far_arrived(which, q)
    far_finish()
    for which in range(4):
        for turn in range(8):
            src, dst, device = piece(which, turn)
            copy = remote(src, dst, send_sem.at[which, turn], recv_sem.at[which, person, head], device)
            if turn == 0:

                @pl.when(owner_core != core)
                def _():
                    copy.wait_send()
            else:
                copy.wait_send()


def attend(
    lists_ref, query_ref, dout_ref, key_ref, value_ref, dkey_zero, dvalue_zero, dquery_ref, dkey_sum, dvalue_sum
):
    first_head = lax.broadcasted_iota(jnp.int32, (BLOCK, PAIR), 1) < HEAD_DIM
    scale = HEAD_DIM ** (-0.5)
    nt = (((1,), (1,)), ((), ()))
    tn = (((0,), (0,)), ((), ()))

    def both_heads(block):
        nothing = jnp.zeros_like(block)
        return [jnp.where(first_head, block, nothing), jnp.where(first_head, nothing, block)]

    def spread(one, two):
        upper = jnp.concatenate(both_heads(one), axis=0)
        lower = jnp.concatenate(both_heads(two), axis=0)
        nothing = jnp.zeros_like(upper)
        return jnp.concatenate(
            [jnp.concatenate([upper, nothing], axis=1), jnp.concatenate([nothing, lower], axis=1)], axis=0
        )

    def load(pair, width):
        blocks = [lists_ref[SLOTS + 1, pair * 2 + i] for i in range(2)]
        lives = [lists_ref[SLOTS, block] for block in blocks]
        q_rows = [pl.ds(pl.multiple_of(block * BLOCK, BLOCK), BLOCK) for block in blocks]
        spots = [
            [pl.ds(pl.multiple_of(lists_ref[slot, block] * BLOCK, BLOCK), BLOCK) for slot in range(width)]
            for block in blocks
        ]
        return lives, q_rows, spots

    def softmax(width, lives, q_rows, spots):
        queries = spread(*[(query_ref[rows, :] * scale).astype(jnp.bfloat16) for rows in q_rows])
        douts = spread(*[dout_ref[rows, :] for rows in q_rows])
        keys = [jnp.concatenate([key_ref[spot, :] for spot in some], axis=0) for some in spots]
        values = [jnp.concatenate([value_ref[spot, :] for spot in some], axis=0) for some in spots]
        both_keys = jnp.concatenate(keys, axis=1)
        both_values = jnp.concatenate(values, axis=1)
        scores = lax.dot_general(both_keys, queries, nt, preferred_element_type=jnp.float32)
        lane = lax.broadcasted_iota(jnp.int32, (1, 2 * PAIR), 1)
        live = jnp.where(lane < PAIR, lives[0], lives[1])
        scores = jnp.concatenate(
            [
                jnp.where(live > slot, scores[slot * BLOCK : (slot + 1) * BLOCK], -1e30)
                for slot in range(width)
            ],
            axis=0,
        )
        top = jnp.max(scores, axis=0, keepdims=True)
        weights = jnp.exp(scores - top)
        d_probs = lax.dot_general(both_values, douts, nt, preferred_element_type=jnp.float32)
        share = 1.0 / jnp.sum(weights, axis=0, keepdims=True)
        delta = jnp.sum(weights * d_probs, axis=0, keepdims=True) * share
        probs = weights * share
        probs_b = probs.astype(jnp.bfloat16)
        d_scores = (probs * (d_probs - delta)).astype(jnp.bfloat16)
        return queries, douts, keys, probs_b, d_scores

    def gradients(q_rows, spots, queries, douts, keys, probs_b, d_scores):
        d_values = jnp.dot(probs_b, douts, preferred_element_type=jnp.float32)
        d_keys = jnp.dot(d_scores, queries, preferred_element_type=jnp.float32)
        for i in range(2):
            lanes = slice(i * PAIR, (i + 1) * PAIR)
            d_queries = lax.dot_general(d_scores[:, lanes], keys[i], tn, preferred_element_type=jnp.float32)
            d_queries = jnp.where(first_head, d_queries[:BLOCK], d_queries[BLOCK:]) * scale
            dquery_ref[q_rows[i], :] = d_queries.astype(jnp.bfloat16)
            for slot, spot in enumerate(spots[i]):
                part = slice(slot * BLOCK, (slot + 1) * BLOCK)
                dvalue_sum[spot, :] += d_values[part, lanes]
                dkey_sum[spot, :] += d_keys[part, lanes]

    def body(group, width):
        loaded = [load(group * GROUP + i, width) for i in range(GROUP)]
        done = [softmax(width, *some) for some in loaded]
        for some, values in zip(loaded, done):
            gradients(*some[1:], *values)

    @pl.loop(0, QBLOCKS // (2 * GROUP))
    def _(group):
        live = lists_ref[SLOTS, lists_ref[SLOTS + 1, group * 2 * GROUP]]
        for width in range(STEP, SLOTS + 1, STEP):

            @pl.when((live <= width) & (live > width - STEP))
            def _():
                body(group, width)


def exchange_out(
    dquery_ref, dkey_ref, dvalue_ref,
    dquery_out, dkey_out, dvalue_out,
    rounded, arrived, far_arrived_buf, total, send_sem, recv_sem, halo_send, halo_recv,
    relay_buf, far_send, far_recv, relay_send, relay_recv,
):
    ctx, head, core, z, group = place()
    near, far, has_far, near_first, far_first = neighbours()
    parts = (dkey_ref, dvalue_ref)

    def round_halo():
        for which in range(2):
            for side in range(2):
                rows = pl.ds(6 * side * PERSON, 2 * PERSON)
                rounded[which, pl.ds(2 * side * PERSON, 2 * PERSON), :] = parts[which][rows, :].astype(jnp.bfloat16)

    greet(round_halo)
    outs = (dquery_out, dkey_out, dvalue_out)

    def halo(which, i):
        spot = 2 - 2 * core + i
        return remote(
            rounded.at[which, pl.ds(pl.multiple_of(spot * PERSON, PERSON), PERSON), :],
            arrived.at[which, i],
            halo_send.at[which, i],
            halo_recv.at[which, i],
            near,
        )

    def far_source(which, q):
        return rounded.at[which, pl.ds(pl.multiple_of(2 * core * PERSON + q * HALF, HALF), HALF), :]

    def far_target(which, q, to_core):
        return far_arrived_buf.at[which, pl.ds(pl.multiple_of(q * HALF, HALF), HALF), :]

    far_start, far_forward, far_arrived, far_finish = far_pieces(
        far_source, far_target, relay_buf, far_send, far_recv, relay_send, relay_recv
    )
    for which in range(2):
        for q in range(4):
            far_start(which, q)
    for which in range(2):
        for i in range(2):
            halo(which, i).start()

    pair = head * 4 + z
    column = pl.multiple_of(pair * PAIR, PAIR)

    def piece(which, who, half):
        src = dquery_ref if which == 0 else total.at[which - 1]
        src = src.at[pl.ds(pl.multiple_of(who * PERSON + half * HALF, HALF), HALF), :]
        return src, outs[which].at[:, pl.ds(column, PAIR)], (group * 8 + core * 4 + who, half)

    def send(which, who, half):
        src, dst, device = piece(which, who, half)
        recv = recv_sem.at[which, pair]
        itself = (device[0] == ctx) & (head == half)

        @pl.when(itself)
        def _():
            pltpu.make_async_copy(src, dst, recv).start()

        @pl.when(jnp.logical_not(itself))
        def _():
            remote(src, dst, send_sem.at[which, who, half], recv, device).start()

    def add(which, side, i):
        who = (far_first if side else near_first) + i
        own = parts[which][pl.ds(pl.multiple_of((2 + who) * PERSON, PERSON), PERSON), :]
        rows = pl.ds(pl.multiple_of(who * PERSON, PERSON), PERSON)
        if not side:
            halo(which, i).wait_recv()
            total[which, rows, :] = (own + arrived[which, i].astype(jnp.float32)).astype(jnp.bfloat16)
            return
        far_arrived(which, 2 * i)
        far_arrived(which, 2 * i + 1)

        @pl.when(has_far)
        def _():
            other = far_arrived_buf[which, pl.ds(i * PERSON, PERSON), :].astype(jnp.float32)
            total[which, rows, :] = (own + other).astype(jnp.bfloat16)

        @pl.when(jnp.logical_not(has_far))
        def _():
            total[which, rows, :] = own.astype(jnp.bfloat16)

    passes_on = relay_role()[0]

    def key_across():
        for i in range(2):
            send(1, near_first + i, 1 - head)

    for who in range(4):
        send(0, who, 1 - head)
        send(0, who, head)
    for i in range(2):
        add(0, 0, i)
        send(1, near_first + i, head)
    pl.when(jnp.logical_not(passes_on))(key_across)
    for which in range(2):
        far_forward(which)
    pl.when(passes_on)(key_across)
    def far_part(which):
        for i in range(2):
            add(which, 1, i)
            send(which + 1, far_first + i, 1 - head)
            send(which + 1, far_first + i, head)

    far_part(0)
    for i in range(2):
        add(1, 0, i)
        send(2, near_first + i, 1 - head)
        send(2, near_first + i, head)
    far_part(1)
    far_finish()
    for which in range(2):
        for i in range(2):
            halo(which, i).wait_send()

    for which in range(3):
        for who in range(4):
            for half in range(2):
                src, dst, device = piece(which, who, half)

                @pl.when((device[0] != ctx) | (head != half))
                def _():
                    remote(
                        src, dst, send_sem.at[which, who, half], recv_sem.at[which, pair], device
                    ).wait_send()

        for source in range(8):
            part = outs[which].at[:, pl.ds(source * PAIR, PAIR)]
            pltpu.make_async_copy(part, part, recv_sem.at[which, source]).wait()


def put_out(dquery_ref, dkey_ref, dvalue_ref, dquery_out, dkey_out, dvalue_out, sem):
    pairs = ((dquery_ref, dquery_out), (dkey_ref, dkey_out), (dvalue_ref, dvalue_out))
    copies = [pltpu.make_async_copy(src, dst, sem.at[i]) for i, (src, dst) in enumerate(pairs)]
    for copy in copies:
        copy.start()
    for copy in copies:
        copy.wait()


def on_device(queries, keys_in, values, d_out, pair_blocks, pair_count):
    hbm = pl.BlockSpec(memory_space=pltpu.HBM)
    vmem = pl.BlockSpec(memory_space=pltpu.VMEM)
    dma = pltpu.SemaphoreType.DMA
    wide = jax.ShapeDtypeStruct((WINDOW * PERSON, PAIR), jnp.bfloat16)
    narrow = jax.ShapeDtypeStruct((LOCAL * PERSON, PAIR), jnp.bfloat16)
    rows = jax.ShapeDtypeStruct(queries.shape, jnp.bfloat16)
    blocks = pair_count.shape[0]
    tables = (pair_blocks.T, pair_count.reshape(1, blocks))
    sources = [
        pltpu.with_memory_space_constraint(x, pltpu.HBM) for x in (keys_in, values, queries, d_out) + tables
    ]
    sums = jax.ShapeDtypeStruct((WINDOW * PERSON, PAIR), jnp.float32)
    keys, vals, query, dout, lists, key_sum, value_sum = pl.pallas_call(
        exchange_in,
        out_shape=(wide, wide, narrow, narrow, jax.ShapeDtypeStruct((LIST_ROWS, 128), jnp.int32), sums, sums),
        in_specs=[hbm] * 6,
        out_specs=(vmem,) * 7,
        scratch_shapes=[
            pltpu.VMEM((SLOTS, blocks), jnp.int32),
            pltpu.VMEM((1, blocks), jnp.int32),
            dma((2,)), dma((4, 8)), dma((4, 4, 2)), dma((2, 2)), dma((2, 2)),
            pltpu.VMEM((2, HALF, PAIR), jnp.bfloat16),
            dma((2, 4)), dma((2, 4)), dma((2,)), dma((2,)),
        ],
        compiler_params=pltpu.CompilerParams(collective_id=0, has_side_effects=True, vmem_limit_bytes=16 << 20),
        name="exchange_in",
    )(*sources)
    d_query, d_key, d_value = pl.pallas_call(
        attend,
        out_shape=(narrow, sums, sums),
        in_specs=[pl.BlockSpec(memory_space=pltpu.SMEM)] + [vmem] * 6,
        out_specs=(vmem,) * 3,
        input_output_aliases={5: 1, 6: 2},
        compiler_params=pltpu.CompilerParams(vmem_limit_bytes=24 << 20),
        name="attend",
    )(lists, query, dout, keys, vals, key_sum, value_sum)
    results = pl.pallas_call(
        exchange_out,
        out_shape=(rows,) * 3,
        in_specs=[vmem] * 3,
        out_specs=(vmem,) * 3,
        scratch_shapes=[
            pltpu.VMEM((2, 4 * PERSON, PAIR), jnp.bfloat16),
            pltpu.VMEM((2, 2, PERSON, PAIR), jnp.bfloat16),
            pltpu.VMEM((2, 2 * PERSON, PAIR), jnp.bfloat16),
            pltpu.VMEM((2, LOCAL * PERSON, PAIR), jnp.bfloat16),
            dma((3, 4, 2)), dma((3, 8)), dma((2, 2)), dma((2, 2)),
            pltpu.VMEM((2, HALF, PAIR), jnp.bfloat16),
            dma((2, 4)), dma((2, 4)), dma((2,)), dma((2,)),
        ],
        compiler_params=pltpu.CompilerParams(collective_id=1, has_side_effects=True, vmem_limit_bytes=16 << 20),
        name="exchange_out",
    )(d_query, d_key, d_value)
    return pl.pallas_call(
        put_out,
        out_shape=(rows,) * 3,
        in_specs=[vmem] * 3,
        out_specs=(hbm,) * 3,
        scratch_shapes=[dma((3,))],
        compiler_params=pltpu.CompilerParams(vmem_limit_bytes=8 << 20),
        name="put_out",
    )(*results)


def solution(mesh):
    tokens = P(("ctx", "head"), None)
    return jax.shard_map(
        on_device,
        mesh=mesh,
        in_specs=(tokens,) * 4 + (P(), P()),
        out_specs=(tokens,) * 3,
        check_vma=False,
    )
```
